32 devices in a mesh: section: 2 (over x), kvp: 16 (over z, y, core).
Axes of the slice: x: 2, y: 2, z: 4, core: 2. Of those that a mesh axis runs over, the one named last changes fastest.
Arguments:
- entering: bfloat16 [2, 8, 8192], P('section', None, 'kvp'), may hold values from -6 to 6
- newcomer: bfloat16 [1, 8, 8192], P(None, None, 'kvp'), may hold values from -6 to 6
- norm_gain: bfloat16 [2, 8192], P('section'), may hold values from 0.25 to 1.75
- query_weight: bfloat16 [2, 8192, 8192], P('section', None, 'kvp'), may hold values from -0.0625 to 0.0625
- keyvalue_weight: bfloat16 [2, 8192, 2048], P('section', None, 'kvp'), may hold values from -0.0625 to 0.0625
- key_cache: bfloat16 [2, 2, 8, 512, 1024], P('section', None, None, 'kvp'), may hold values from -96 to 96
- value_cache: bfloat16 [2, 2, 8, 512, 1024], P('section', None, None, 'kvp'), may hold values from -6 to 6
- cache_lengths: int32 [3, 8], replicated, may hold values from 1 to 512, as said below
Outputs:
- layer_outputs: bfloat16 [2, 2, 8, 8192], P('section', None, None, 'kvp')
The draws below stay inside these ranges and needn't reach their ends.
Inputs may be any that keep to these rules, and one draw needn't show every extreme that they name: `cache_lengths`: in every micro-batch some request has exactly 512 cached positions.
All inputs are finite; a program needn't handle non-finite values.
Results may differ from the reference program's by a relative error of at most 0.024.
The reference program's roundings to bfloat16 on the way count: a program that leaves them out, or rounds other values in their place, can miss the bound.
Values may be sent and summed in bfloat16 or wider, within the bound.
A program may use at most 128 MiB of HBM per device.

```python
import math
import jax
import jax.numpy as jnp
from jax import lax

D = 8192
NH = 64
KVH = 8
HD = 128
REQ = 8
TICKS = 2
CTX = 512
LAYERS = 2
MICRO = 3


def draw_key_cache(key, part):
    shape = (LAYERS, TICKS, REQ, CTX, KVH, HD)
    second_key = jax.random.fold_in(jax.random.fold_in(key, 11), 1)
    values = jnp.clip(jax.random.normal(second_key, shape, dtype=jnp.float32), -6.0, 6.0)
    return values.reshape(LAYERS, TICKS, REQ, CTX, KVH * HD).astype(jnp.bfloat16)


def draw_cache_lengths(key, part):
    first_key, second_key = jax.random.split(jax.random.fold_in(key, 23))
    drawn = jax.random.randint(first_key, (MICRO, REQ), 1, CTX + 1)
    chosen = jax.random.randint(second_key, (MICRO, 1), 0, REQ)
    longest = jnp.arange(REQ, dtype=jnp.int32)[None, :] == chosen
    return jnp.where(longest, CTX, drawn).astype(jnp.int32)


def shard_levels(key, shape, pieces, least, top_value):
    def one(dim, blocks):
        heights = jax.random.uniform(jax.random.fold_in(jax.random.fold_in(key, 6), dim), (blocks,), jnp.float32, least / len(pieces), top_value / len(pieces))
        return jnp.repeat(jnp.exp(heights), shape[dim] // blocks).reshape((-1,) + (1,) * (len(shape) - dim - 1))

    loudness = one(*pieces[0])
    for cut in pieces[1:]:
        loudness = loudness * one(*cut)
    return loudness


def gaussian(rng, dims, scale, most, pieces=(), kind=jnp.bfloat16):
    loudness = shard_levels(rng, dims, pieces, -0.22, 0.18) if pieces else 1.0
    entries = jax.random.normal(rng, dims, jnp.float32) * scale * loudness
    return jnp.minimum(jnp.maximum(entries, -most), most).astype(kind)


def setup_inputs(seed: int = 0) -> dict:
    streams_of = jax.random.split(jax.random.key(seed), 9)
    return {
        "entering": gaussian(streams_of[0], (LAYERS, REQ, D), 1.0, 6.0, ((0, 2), (2, 16))),
        "newcomer": gaussian(streams_of[1], (TICKS - 1, REQ, D), 1.0, 6.0, ((2, 16),)),
        "norm_gain": jnp.clip(1.0 + 0.15 * jax.random.normal(streams_of[2], (LAYERS, D), jnp.float32), 0.25, 1.75).astype(jnp.bfloat16),
        "query_weight": gaussian(streams_of[3], (LAYERS, D, NH * HD), D ** -0.5, 0.0625, ((0, 2), (2, 16))),
        "keyvalue_weight": gaussian(streams_of[4], (LAYERS, D, 2 * KVH * HD), D ** -0.5, 0.0625, ((0, 2), (2, 16))),
        "key_cache": draw_key_cache(jax.random.fold_in(streams_of[8], 71), 0),
        "value_cache": gaussian(streams_of[6], (LAYERS, TICKS, REQ, CTX, KVH * HD), 1.0, 6.0, ((0, 2), (3, 16))),
        "cache_lengths": draw_cache_lengths(jax.random.fold_in(streams_of[8], 71), 0),
    }


def rotate(values, positions):
    half_width = values.shape[-1] // 2
    exponent = jnp.arange(half_width, dtype=jnp.float32) * (2.0 / values.shape[-1])
    frequency = jnp.power(jnp.float32(500000.0), -exponent)
    angles = positions.astype(jnp.float32)[:, None, None] * frequency
    cosine = jnp.cos(angles)
    sine = jnp.sin(angles)
    first = values[..., :half_width]
    second = values[..., half_width:]
    return jnp.concatenate([first * cosine - second * sine, second * cosine + first * sine], axis=-1)

def section_layer(hidden, gain, query_w, keyvalue_w, cached_keys, cached_values, lengths_now):
    x_float = hidden.astype(jnp.float32)
    mean_square = lax.optimization_barrier(jnp.mean(x_float * x_float, axis=-1, keepdims=True))
    normed = (x_float * lax.rsqrt(mean_square + 1e-05) * gain.astype(jnp.float32)).astype(jnp.bfloat16)
    query = jnp.dot(normed, query_w, preferred_element_type=jnp.float32).reshape(REQ, NH, HD)
    query = rotate(query, lengths_now).astype(jnp.bfloat16)
    fresh = jnp.dot(normed, keyvalue_w, preferred_element_type=jnp.float32).astype(jnp.bfloat16)
    new_key = rotate(fresh[:, :KVH * HD].reshape(REQ, KVH, HD).astype(jnp.float32), lengths_now)
    new_value = fresh[:, KVH * HD:].reshape(REQ, KVH, HD).astype(jnp.float32)
    grouped = query.astype(jnp.float32).reshape(REQ, KVH, NH // KVH, HD)
    key_float = cached_keys.astype(jnp.float32).reshape(REQ, CTX, KVH, HD)
    value_float = cached_values.astype(jnp.float32).reshape(REQ, CTX, KVH, HD)
    score_scale = 1.0 / math.sqrt(HD)
    scores = jnp.einsum('bgrd,bpgd->bgrp', grouped, key_float) * score_scale
    in_cache = (jnp.arange(CTX, dtype=jnp.int32)[None, :] < lengths_now[:, None])[:, None, None, :]
    scores = jnp.where(in_cache, scores, jnp.float32(-1e+30))
    new_score = jnp.einsum('bgrd,bgd->bgr', grouped, new_key) * score_scale
    cache_max = lax.optimization_barrier(jnp.max(scores, axis=-1))
    top_score = jnp.maximum(cache_max, new_score)
    weights = jnp.where(in_cache, jnp.exp(scores - cache_max[..., None]), jnp.float32(0.0))
    value_weights = weights.astype(jnp.bfloat16).astype(jnp.float32)
    old_factor = jnp.exp(cache_max - top_score)
    new_weight = jnp.exp(new_score - top_score)
    denominator = lax.optimization_barrier(jnp.sum(weights, axis=-1)) * old_factor + new_weight
    weighted = jnp.einsum('bgrp,bpgd->bgrd', value_weights, value_float)
    numerator = weighted * old_factor[..., None] + new_weight[..., None] * new_value[:, :, None, :]
    attended = (numerator / denominator[..., None]).reshape(REQ, NH * HD)
    return (x_float + attended).astype(jnp.bfloat16)

def reference(entering, newcomer, norm_gain, query_weight, keyvalue_weight, key_cache, value_cache, cache_lengths):
    results = []
    for layer_index in range(LAYERS):
        results.append([None] * TICKS)
    for tick in range(TICKS):
        for layer_index in range(LAYERS):
            if tick == 0:
                hidden = entering[layer_index]
            elif layer_index == 0:
                hidden = newcomer[tick - 1]
            else:
                hidden = results[layer_index - 1][tick - 1]
            micro_id = tick + (LAYERS - 1 - layer_index)
            lengths_now = cache_lengths[micro_id]
            results[layer_index][tick] = section_layer(hidden, norm_gain[layer_index], query_weight[layer_index], keyvalue_weight[layer_index], key_cache[layer_index, tick], value_cache[layer_index, tick], lengths_now)
    return jnp.stack([jnp.stack(row, axis=0) for row in results], axis=0)
```

```python
import functools
import math

import jax
import jax.numpy as jnp
from jax import lax
from jax.experimental import pallas as pl
from jax.experimental.pallas import tpu as pltpu
from jax.sharding import PartitionSpec as P

NH = 64
KVH = 8
HD = 128
GROUP = NH // KVH
THETA = 500000.0
EPS = 1e-05
NEG = -1e30
LEAST = -1e29
MESH = pl.DeviceIdType.MESH
F32 = jnp.float32
BF16 = jnp.bfloat16
SPLITS = (2, 2)


def layer_kernel(
    n,
    sections,
    lengths_ref,
    entering_ref,
    newcomer_ref,
    gain_hbm,
    query_hbm,
    keyvalue_hbm,
    keys_hbm,
    values_hbm,
    out_ref,
    query_w,
    keyvalue_w,
    gain,
    inputs,
    normed,
    own_heads_out,
    heads,
    fresh_out,
    fresh_heads,
    staged,
    parts,
    leaving,
    load_sem,
    weight_sem,
    cache_sem,
    cache_send,
    send_sem,
    recv_sem,
    heads_sem,
    ready_sem,
    *caches,
):
    ticks, rows, width = out_ref.shape
    keys, values = caches[:ticks], caches[ticks:]
    features = query_w.shape[0]
    own_heads = NH // n
    own_rows = own_heads * rows
    kv_width = keyvalue_w.shape[1]
    pieces = HD // kv_width
    per_group = n // KVH
    span = keys_hbm.shape[1] // rows
    chunks = weight_sem.shape[0] - 1
    depth = features // chunks
    scale = 1.0 / math.sqrt(HD)
    stride = HD // own_heads

    section = lax.axis_index("section")
    me = lax.axis_index("kvp")

    def peer(step, skip):
        j = jnp.where(me >= n // 2, step, n - 1 - skip - step)
        return j + (j >= me).astype(jnp.int32) if skip else j

    barrier = pltpu.get_barrier_semaphore()

    def greet(step, carry):
        pl.semaphore_signal(
            barrier, inc=1, device_id=(section, peer(step, 1)), device_id_type=MESH
        )
        return carry

    lax.fori_loop(0, n - 1, greet, 0)
    if sections > 1:

        @pl.when(section < sections - 1)
        def _():
            pl.semaphore_signal(barrier, inc=1, device_id=(section + 1, me), device_id_type=MESH)

        @pl.when(section > 0)
        def _():
            pl.semaphore_signal(barrier, inc=1, device_id=(section - 1, me), device_id_type=MESH)

    own_load = pltpu.make_async_copy(entering_ref, inputs.at[0, me], load_sem.at[1])
    own_load.start()
    weight_loads = []
    for c in range(chunks):
        part = pl.ds(c * depth, depth)
        weight_loads.append(
            pltpu.make_async_copy(query_hbm.at[part], query_w.at[part], weight_sem.at[c])
        )
        weight_loads[-1].start()
    gain_load = pltpu.make_async_copy(gain_hbm, gain, load_sem.at[0])
    gain_load.start()
    weight_loads.append(pltpu.make_async_copy(keyvalue_hbm, keyvalue_w, weight_sem.at[chunks]))
    weight_loads[-1].start()

    neighbours = (section > 0).astype(jnp.int32) + (section < sections - 1).astype(jnp.int32)
    pl.semaphore_wait(barrier, n - 1 + neighbours)
    if sections > 1:

        @pl.when(section > 0)
        def _():
            pl.semaphore_signal(ready_sem, inc=1, device_id=(section - 1, me), device_id_type=MESH)

    def remote(source, target, sent, received, to_section, to):
        return pltpu.make_async_remote_copy(
            src_ref=source,
            dst_ref=target,
            send_sem=sent,
            recv_sem=received,
            device_id=(to_section, to),
            device_id_type=MESH,
        )

    def deliver(source, target, sent, received, to):
        @pl.when(to != me)
        def _():
            remote(source, target, sent, received, section, to).start()

        @pl.when(to == me)
        def _():
            pltpu.make_async_copy(source, target, received).start()

    def spread(source, target, sent, received):
        def send(step, carry):
            remote(source, target, sent, received, section, peer(step, 1)).start()
            return carry

        lax.fori_loop(0, n - 1, send, 0)

    def arrived(buffer, count, sem):
        if count:
            whole = buffer.at[pl.ds(0, count)]
            pltpu.make_async_copy(whole, whole, sem).wait()

    def all_sent(buffer, count, at_home, sem):
        @pl.when(at_home)
        def _():
            arrived(buffer, count - 1, sem)

        @pl.when(jnp.logical_not(at_home))
        def _():
            arrived(buffer, count, sem)

    def deal_caches(t):
        split = SPLITS[t]
        share = keys_hbm.shape[2] // split
        member = lax.rem(me, split)
        first = me - member
        for kind, (source, target) in enumerate(((keys_hbm, keys[t]), (values_hbm, values[t]))):
            for i in range(1, split):
                other = lax.rem(member + i, split)
                columns = pl.ds(pl.multiple_of(other * share, share), share)
                remote(
                    source.at[t, :, columns],
                    target.at[member],
                    cache_send.at[t, kind],
                    cache_sem.at[t, kind],
                    section,
                    first + other,
                ).start()
            columns = pl.ds(pl.multiple_of(member * share, share), share)
            pltpu.make_async_copy(
                source.at[t, :, columns], target.at[member], cache_sem.at[t, kind]
            ).start()

    spread(entering_ref, inputs.at[0, me], send_sem.at[0, 0], recv_sem.at[0, 0])
    for t in range(ticks):
        deal_caches(t)

    lane = lax.broadcasted_iota(jnp.int32, (rows, HD), 1)
    row = lax.broadcasted_iota(jnp.int32, (rows, HD), 0)
    half = HD // 2
    exponent = (lane % half).astype(F32) * (2.0 / HD)
    frequency = jnp.exp(exponent * (-math.log(THETA)))
    turns = []
    biases = []
    for t in range(ticks):
        split = SPLITS[t]
        reach = split * rows * span
        micro = t + sections - 1 - section
        place = lax.broadcasted_iota(jnp.int32, (rows, reach), 1)
        request = lax.broadcasted_iota(jnp.int32, (rows, reach), 0)
        slot = place // (rows * span)
        position = (me // split * split + slot) * span + place % span
        by_row = jnp.zeros((rows, HD), jnp.int32)
        limit = jnp.zeros((rows, reach), jnp.int32)
        for b in range(rows):
            length = lengths_ref[micro, b]
            by_row = jnp.where(row == b, length, by_row)
            limit = jnp.where(request == b, length, limit)
        angles = by_row.astype(F32) * frequency
        sine = jnp.sin(angles)
        turns.append((jnp.cos(angles), jnp.where(lane < half, -sine, sine)))
        valid = (place // span % rows == request) & (position < limit)
        biases.append(jnp.where(valid, 0.0, NEG).astype(F32))

    def rotated(head, t):
        cosine, sine = turns[t]
        return head * cosine + pltpu.roll(head, half, 1) * sine

    def packed(tops, totals):
        p = jnp.zeros((rows, HD), F32)
        for h in range(own_heads):
            p = jnp.where(lane == h * stride, tops[h], p)
            if totals is not None:
                p = jnp.where(lane == h * stride + 3, totals[h], p)
        return p

    kinds = n // 2
    fresh_group = (me % kinds) // pieces
    fresh_slot = (me // kinds) * pieces + me % pieces
    own_group = me // per_group

    gain_load.wait()
    for t in range(ticks):
        split = SPLITS[t]
        owners = n // split
        held = KVH // split
        reach = split * rows * span
        member = lax.rem(me, split)
        cluster = me // split
        if t == 0:
            own_load.wait()
            arrived(inputs.at[0], n - 1, recv_sem.at[0, 0])
        else:
            arrived(inputs.at[t], n, recv_sem.at[t, 0])

        squares = jnp.zeros((rows, width), F32)
        for s in range(n):
            x = inputs[t, s].astype(F32)
            squares = squares + x * x
        mean_square = jnp.sum(squares, axis=-1, keepdims=True) * (1.0 / features)
        factor = lax.rsqrt(mean_square + EPS)
        for s in range(n):
            part = pl.ds(s * width, width)
            x = inputs[t, s].astype(F32)
            normed[:, part] = (x * factor * gain[:, part].astype(F32)).astype(BF16)

        query = jnp.zeros((rows, width), F32)
        for c in range(chunks):
            part = pl.ds(c * depth, depth)
            if t == 0:
                weight_loads[c].wait()
            query = query + jnp.dot(normed[:, part], query_w[part], preferred_element_type=F32)
        own_query = jnp.concatenate(
            [rotated(query[:, h * HD : (h + 1) * HD], t) for h in range(own_heads)], axis=0
        ).astype(BF16)
        own_heads_out[t] = own_query
        own_query = own_query.astype(F32)
        home = me // owners
        slot = lax.rem(me, owners)

        def send_heads(step, carry):
            to = jnp.where(cluster >= owners // 2, step, owners - 1 - step) * split + home
            deliver(
                own_heads_out.at[t],
                heads.at[t, slot],
                send_sem.at[t, 1],
                heads_sem.at[t, slot // per_group],
                to,
            )
            return carry

        lax.fori_loop(0, owners, send_heads, 0)

        if t == 0:
            weight_loads[chunks].wait()
        fresh = jnp.dot(normed[...], keyvalue_w[...], preferred_element_type=F32).astype(BF16)
        if pieces > 1:
            fresh = jnp.concatenate([fresh.astype(F32)] * pieces, axis=1)
            fresh = jnp.where(lane // kv_width == me % pieces, fresh, 0.0).astype(BF16)
        fresh_out[t] = fresh
        for j in range(per_group):
            deliver(
                fresh_out.at[t],
                fresh_heads.at[t, fresh_slot],
                send_sem.at[t, 4],
                recv_sem.at[t, 1],
                fresh_group * per_group + j,
            )

        if t == 0:
            @pl.when(section == 0)
            def _():
                for u in range(1, ticks):
                    pltpu.make_async_copy(
                        newcomer_ref.at[u - 1], inputs.at[u, me], recv_sem.at[u, 0]
                    ).start()
                    spread(
                        newcomer_ref.at[u - 1], inputs.at[u, me], send_sem.at[u, 0], recv_sem.at[u, 0]
                    )

        arrived(keys[t], split, cache_sem.at[t, 0])
        bias = biases[t]
        for i in range(held):
            kv = jnp.where(me >= member * owners + owners // 2, held - 1 - i, i)
            arrived(heads.at[t], per_group, heads_sem.at[t, kv])
            queries = jnp.concatenate(
                [heads[t, kv * per_group + j].astype(F32) for j in range(per_group)], axis=0
            ).astype(BF16)
            columns = pl.ds(pl.multiple_of(kv * HD, HD), HD)
            scores = lax.dot_general(
                queries,
                keys[t][:, :, columns].reshape(reach, HD),
                (((1,), (1,)), ((), ())),
                preferred_element_type=F32,
            )
            scores = scores.reshape(GROUP, rows, reach) * scale + bias[None]
            top = jnp.maximum(jnp.max(scores, axis=-1, keepdims=True), LEAST)
            weights = jnp.exp(scores - top)
            total = jnp.sum(weights, axis=-1, keepdims=True)
            if i == 0:
                arrived(values[t], split, cache_sem.at[t, 1])
            weighted = jnp.dot(
                weights.reshape(GROUP * rows, reach).astype(BF16),
                values[t][:, :, columns].reshape(reach, HD),
                preferred_element_type=F32,
            )
            for j in range(per_group):
                these = slice(j * own_heads, (j + 1) * own_heads)
                stats = packed(top[these], total[these])
                high = stats.astype(BF16).astype(F32)
                rest = stats - high
                middle = rest.astype(BF16).astype(F32)
                stats = high + pltpu.roll(middle, 1, 1) + pltpu.roll(rest - middle, 2, 1)
                place = kv * per_group + j
                staged[t, place] = jnp.concatenate(
                    [weighted[j * own_rows : (j + 1) * own_rows], stats], axis=0
                ).astype(BF16)
                deliver(
                    staged.at[t, place],
                    parts.at[t, cluster],
                    send_sem.at[t, 2],
                    recv_sem.at[t, 2],
                    member * owners + place,
                )

        arrived(fresh_heads.at[t], 2 * pieces, recv_sem.at[t, 1])
        new_key = jnp.zeros((rows, HD), F32)
        new_value = jnp.zeros((rows, HD), F32)
        for j in range(pieces):
            new_key = new_key + fresh_heads[t, j].astype(F32)
            new_value = new_value + fresh_heads[t, pieces + j].astype(F32)
        new_key = rotated(new_key, t)
        new_score = packed(
            [
                jnp.sum(own_query[h * rows : (h + 1) * rows] * new_key, axis=-1, keepdims=True)
                * scale
                for h in range(own_heads)
            ],
            None,
        )

        arrived(parts.at[t], owners, recv_sem.at[t, 2])
        sums = []
        blocks = []
        for s in range(owners):
            block = parts[t, s].astype(F32)
            blocks.append(block)
            stats = block[own_rows : own_rows + rows]
            sums.append(stats + pltpu.roll(stats, HD - 1, 1) + pltpu.roll(stats, HD - 2, 1))
        top = new_score
        for s in range(owners):
            top = jnp.maximum(top, sums[s])
        new_weight = jnp.exp(new_score - top)
        denominator = new_weight
        factors = []
        for s in range(owners):
            factors.append(jnp.exp(sums[s] - top))
            denominator = denominator + factors[s] * pltpu.roll(sums[s], HD - 3, 1)
        inverse = 1.0 / denominator
        attended = []
        for h in range(own_heads):
            at = slice(h * stride, h * stride + 1)
            total = (new_weight * inverse)[:, at] * new_value
            for s in range(owners):
                total = total + (factors[s] * inverse)[:, at] * blocks[s][h * rows : (h + 1) * rows]
            attended.append(total)
        attended = jnp.concatenate(attended, axis=1)
        result = (inputs[t, me].astype(F32) + attended).astype(BF16)
        out_ref[t] = result
        if t < ticks - 1 and sections > 1:
            leaving[t] = result

            @pl.when(section < sections - 1)
            def _():
                if t == 0:
                    pl.semaphore_wait(ready_sem, 1)

                def send(step, carry):
                    remote(
                        leaving.at[t],
                        inputs.at[t + 1, me],
                        send_sem.at[t, 3],
                        recv_sem.at[t + 1, 0],
                        section + 1,
                        peer(step, 0),
                    ).start()
                    return carry

                lax.fori_loop(0, n, send, 0)

    for t in range(ticks):
        split = SPLITS[t]
        owners = n // split
        if t == 0:
            arrived(inputs.at[t], n - 1, send_sem.at[t, 0])
        else:

            @pl.when(section == 0)
            def _():
                arrived(inputs.at[t], n - 1, send_sem.at[t, 0])

        inside = lax.rem(me, split) == me // owners
        all_sent(heads.at[t], owners, inside, send_sem.at[t, 1])
        all_sent(parts.at[t], owners, inside, send_sem.at[t, 2])
        all_sent(fresh_heads.at[t], per_group, fresh_group == own_group, send_sem.at[t, 4])
        for kind in range(2):
            arrived((keys, values)[kind][t], split - 1, cache_send.at[t, kind])
        if t < ticks - 1 and sections > 1:

            @pl.when(section < sections - 1)
            def _():
                arrived(inputs.at[t], n, send_sem.at[t, 3])


def shards(
    n,
    sections,
    entering,
    newcomer,
    norm_gain,
    query_weight,
    keyvalue_weight,
    key_cache,
    value_cache,
    cache_lengths,
):
    _, rows, width = entering.shape
    _, features, _ = query_weight.shape
    kv_width = keyvalue_weight.shape[2]
    _, ticks, _, span, kv_features = key_cache.shape
    own_rows = (NH // n) * rows
    pieces = HD // kv_width
    per_group = n // KVH
    chunks = 4
    most = n // min(SPLITS)
    anywhere = pl.BlockSpec(memory_space=pl.ANY)
    dealt = [pltpu.VMEM((g, rows * span, kv_features // g), BF16) for g in SPLITS]
    out = pl.pallas_call(
        functools.partial(layer_kernel, n, sections),
        out_shape=jax.ShapeDtypeStruct((ticks, rows, width), BF16),
        in_specs=[pl.BlockSpec(memory_space=pltpu.SMEM)] + [anywhere] * 7,
        out_specs=pl.BlockSpec(memory_space=pltpu.VMEM),
        scratch_shapes=[
            pltpu.VMEM((features, width), BF16),
            pltpu.VMEM((features, kv_width), BF16),
            pltpu.VMEM((1, features), BF16),
            pltpu.VMEM((ticks, n, rows, width), BF16),
            pltpu.VMEM((rows, features), BF16),
            pltpu.VMEM((ticks, own_rows, HD), BF16),
            pltpu.VMEM((ticks, most, own_rows, HD), BF16),
            pltpu.VMEM((ticks, rows, HD), BF16),
            pltpu.VMEM((ticks, max(2 * pieces, per_group), rows, HD), BF16),
            pltpu.VMEM((ticks, most, own_rows + rows, HD), BF16),
            pltpu.VMEM((ticks, most, own_rows + rows, HD), BF16),
            pltpu.VMEM((ticks, rows, width), BF16),
            pltpu.SemaphoreType.DMA((2,)),
            pltpu.SemaphoreType.DMA((chunks + 1,)),
            pltpu.SemaphoreType.DMA((ticks, 2)),
            pltpu.SemaphoreType.DMA((ticks, 2)),
            pltpu.SemaphoreType.DMA((ticks, 5)),
            pltpu.SemaphoreType.DMA((ticks, 3)),
            pltpu.SemaphoreType.DMA((ticks, KVH // min(SPLITS))),
            pltpu.SemaphoreType.REGULAR,
        ]
        + dealt
        + dealt,
        compiler_params=pltpu.CompilerParams(
            collective_id=0, has_side_effects=True, vmem_limit_bytes=60 << 20
        ),
    )(
        cache_lengths,
        entering[0],
        newcomer,
        norm_gain,
        query_weight[0],
        keyvalue_weight[0],
        key_cache.reshape(ticks, rows * span, kv_features),
        value_cache.reshape(ticks, rows * span, kv_features),
    )
    return out[None]


def solution(mesh):
    placed = (
        P("section", None, "kvp"),
        P(None, None, "kvp"),
        P("section", None),
        P("section", None, "kvp"),
        P("section", None, "kvp"),
        P("section", None, None, "kvp", None),
        P("section", None, None, "kvp", None),
        P(),
    )
    return jax.shard_map(
        functools.partial(shards, mesh.shape["kvp"], mesh.shape["section"]),
        mesh=mesh,
        in_specs=placed,
        out_specs=P("section", None, None, "kvp"),
        check_vma=False,
    )
```

```python
import functools
import math

import jax
import jax.numpy as jnp
from jax import lax
from jax.experimental import pallas as pl
from jax.experimental.pallas import tpu as pltpu
from jax.sharding import PartitionSpec as P

NH = 64
KVH = 8
HD = 128
GROUP = NH // KVH
THETA = 500000.0
EPS = 1e-05
NEG = -1e30
LEAST = -1e29
MESH = pl.DeviceIdType.MESH
F32 = jnp.float32
BF16 = jnp.bfloat16
NEAR = 2
WIDE = 8


def layer_kernel(
    n,
    sections,
    lengths_hbm,
    entering_ref,
    newcomer_ref,
    gain_hbm,
    query_hbm,
    keyvalue_hbm,
    keys_hbm,
    values_hbm,
    out_ref,
    query_w,
    keyvalue_w,
    gain,
    inputs,
    normed,
    own_heads_out,
    heads,
    fresh_out,
    fresh_heads,
    staged,
    parts,
    leaving,
    load_sem,
    weight_sem,
    cache_sem,
    cache_send,
    send_sem,
    recv_sem,
    heads_sem,
    ready_sem,
    bias_near,
    bias_wide,
    keys_near,
    values_near,
    keys_wide,
    values_wide,
    lengths_ref,
):
    ticks, rows, width = out_ref.shape
    features = query_w.shape[0]
    own_heads = NH // n
    own_rows = own_heads * rows
    kv_width = keyvalue_w.shape[1]
    pieces = HD // kv_width
    per_group = n // KVH
    span = keys_hbm.shape[1] // rows
    chunks = weight_sem.shape[0] - 1
    depth = features // chunks
    scale = 1.0 / math.sqrt(HD)
    stride = HD // own_heads

    section = lax.axis_index("section")
    me = lax.axis_index("kvp")

    own_group = me // per_group

    def peer(step, skip):
        j = jnp.where(me >= n // 2, step, n - 1 - skip - step)
        return j + (j >= me).astype(jnp.int32) if skip else j

    barrier = pltpu.get_barrier_semaphore()

    def greet(step, carry):
        pl.semaphore_signal(
            barrier, inc=1, device_id=(section, peer(step, 1)), device_id_type=MESH
        )
        return carry

    lax.fori_loop(0, n - 1, greet, 0)
    if sections > 1:

        @pl.when(section < sections - 1)
        def _():
            pl.semaphore_signal(barrier, inc=1, device_id=(section + 1, me), device_id_type=MESH)

        @pl.when(section > 0)
        def _():
            pl.semaphore_signal(barrier, inc=1, device_id=(section - 1, me), device_id_type=MESH)

    lengths_load = pltpu.make_async_copy(lengths_hbm, lengths_ref, load_sem.at[2])
    lengths_load.start()
    own_load = pltpu.make_async_copy(entering_ref, inputs.at[0, me], load_sem.at[1])
    own_load.start()
    weight_loads = []
    for c in range(chunks):
        part = pl.ds(c * depth, depth)
        weight_loads.append(
            pltpu.make_async_copy(query_hbm.at[part], query_w.at[part], weight_sem.at[c])
        )
        weight_loads[-1].start()
    gain_load = pltpu.make_async_copy(gain_hbm, gain, load_sem.at[0])
    gain_load.start()
    weight_loads.append(pltpu.make_async_copy(keyvalue_hbm, keyvalue_w, weight_sem.at[chunks]))
    weight_loads[-1].start()

    neighbours = (section > 0).astype(jnp.int32) + (section < sections - 1).astype(jnp.int32)
    pl.semaphore_wait(barrier, n - 1 + neighbours)
    if sections > 1:

        @pl.when(section > 0)
        def _():
            pl.semaphore_signal(ready_sem, inc=1, device_id=(section - 1, me), device_id_type=MESH)

    def remote(source, target, sent, received, to_section, to):
        return pltpu.make_async_remote_copy(
            src_ref=source,
            dst_ref=target,
            send_sem=sent,
            recv_sem=received,
            device_id=(to_section, to),
            device_id_type=MESH,
        )

    def deliver(source, target, sent, received, to):
        @pl.when(to != me)
        def _():
            remote(source, target, sent, received, section, to).start()

        @pl.when(to == me)
        def _():
            pltpu.make_async_copy(source, target, received).start()

    def spread(source, target, sent, received):
        def send(step, carry):
            remote(source, target, sent, received, section, peer(step, 1)).start()
            return carry

        lax.fori_loop(0, n - 1, send, 0)

    def arrived(buffer, count, sem):
        if count:
            whole = buffer.at[pl.ds(0, count)]
            pltpu.make_async_copy(whole, whole, sem).wait()

    def all_sent(buffer, count, at_home, sem):
        @pl.when(at_home)
        def _():
            arrived(buffer, count - 1, sem)

        @pl.when(jnp.logical_not(at_home))
        def _():
            arrived(buffer, count, sem)

    def group_of(member, i, split):
        if split == KVH:
            return member // 2 + lax.rem(member, 2) * (KVH // 2)
        return member * (KVH // split) + i

    def member_of(group, split):
        if split == KVH:
            return lax.rem(group, KVH // 2) * 2 + group // (KVH // 2)
        return group // (KVH // split)

    def owner_slot(group, split):
        return lax.rem(group, KVH // split)

    def cache_of(t, split):
        if split == NEAR:
            return keys_near.at[t], values_near.at[t], bias_near.at[t]
        return keys_wide.at[t - 1], values_wide.at[t - 1], bias_wide.at[t - 1]

    def by_section(t, body):
        if t == 0:
            body(NEAR)
        else:
            pl.when(section == 0)(lambda: body(NEAR))
            if sections > 1:
                pl.when(section > 0)(lambda: body(WIDE))

    def deal_caches(t, split):
        share = keys_hbm.shape[2] // split
        member = lax.rem(me, split)
        first = me - member
        for kind, source in enumerate((keys_hbm, values_hbm)):
            target = cache_of(t, split)[kind]
            for i in range(1, split):
                other = lax.rem(member + i, split)
                columns = pl.ds(
                    pl.multiple_of(group_of(other, 0, split) * HD, HD), share
                )
                remote(
                    source.at[t, :, columns],
                    target.at[member],
                    cache_send.at[t, kind],
                    cache_sem.at[t, kind],
                    section,
                    first + other,
                ).start()
            columns = pl.ds(pl.multiple_of(group_of(member, 0, split) * HD, HD), share)
            pltpu.make_async_copy(
                source.at[t, :, columns], target.at[member], cache_sem.at[t, kind]
            ).start()

    spread(entering_ref, inputs.at[0, me], send_sem.at[0, 0], recv_sem.at[0, 0])
    for t in range(ticks):
        by_section(t, functools.partial(deal_caches, t))

    lane = lax.broadcasted_iota(jnp.int32, (rows, HD), 1)
    half = HD // 2
    exponent = (lane % half).astype(F32) * (2.0 / HD)
    frequency = jnp.exp(exponent * (-math.log(THETA)))
    lengths_load.wait()

    def lengths_of(t, shape):
        request = lax.broadcasted_iota(jnp.int32, shape, 0)
        lengths = jnp.zeros(shape, jnp.int32)
        for b in range(rows):
            length = lengths_ref[t + sections - 1 - section, b]
            lengths = jnp.where(request == b, length, lengths)
        return request, lengths

    def put_bias(t, split):
        shape = (rows, split * rows * span)
        request, limit = lengths_of(t, shape)
        place = lax.broadcasted_iota(jnp.int32, shape, 1)
        slot = place // (rows * span)
        position = (me // split * split + slot) * span + place % span
        valid = (place // span % rows == request) & (position < limit)
        cache_of(t, split)[2][...] = jnp.where(valid, 0.0, NEG).astype(F32)

    turns = []
    for t in range(ticks):
        angles = lengths_of(t, (rows, HD))[1].astype(F32) * frequency
        sine = jnp.sin(angles)
        turns.append((jnp.cos(angles), jnp.where(lane < half, -sine, sine)))
        by_section(t, functools.partial(put_bias, t))

    def rotated(head, t):
        cosine, sine = turns[t]
        return head * cosine + pltpu.roll(head, half, 1) * sine

    def packed(tops, totals):
        p = jnp.zeros((rows, HD), F32)
        for h in range(own_heads):
            p = jnp.where(lane == h * stride, tops[h], p)
            if totals is not None:
                p = jnp.where(lane == h * stride + 3, totals[h], p)
        return p

    kinds = n // 2
    fresh_group = (me % kinds) // pieces
    fresh_slot = (me // kinds) * pieces + me % pieces

    gain_load.wait()
    for t in range(ticks):
        if t == 0:
            own_load.wait()
            arrived(inputs.at[0], n - 1, recv_sem.at[0, 0])
        else:
            arrived(inputs.at[t], n, recv_sem.at[t, 0])

        squares = jnp.zeros((rows, width), F32)
        for s in range(n):
            x = inputs[t, s].astype(F32)
            squares = squares + x * x
        mean_square = jnp.sum(squares, axis=-1, keepdims=True) * (1.0 / features)
        factor = lax.rsqrt(mean_square + EPS)
        for s in range(n):
            part = pl.ds(s * width, width)
            x = inputs[t, s].astype(F32)
            normed[:, part] = (x * factor * gain[:, part].astype(F32)).astype(BF16)

        query = jnp.zeros((rows, width), F32)
        for c in range(chunks):
            part = pl.ds(c * depth, depth)
            if t == 0:
                weight_loads[c].wait()
            query = query + jnp.dot(normed[:, part], query_w[part], preferred_element_type=F32)
        own_query = jnp.concatenate(
            [rotated(query[:, h * HD : (h + 1) * HD], t) for h in range(own_heads)], axis=0
        ).astype(BF16)
        own_heads_out[t] = own_query
        own_query = own_query.astype(F32)
        def send_heads(split):
            owners = n // split
            cluster = me // split
            home = member_of(own_group, split)
            slot = owner_slot(own_group, split) * per_group + lax.rem(me, per_group)

            def send(step, carry):
                to = jnp.where(cluster >= owners // 2, step, owners - 1 - step) * split + home
                deliver(
                    own_heads_out.at[t],
                    heads.at[t, slot],
                    send_sem.at[t, 1],
                    heads_sem.at[t, slot // per_group],
                    to,
                )
                return carry

            lax.fori_loop(0, owners, send, 0)

        by_section(t, send_heads)

        if t == 0:
            weight_loads[chunks].wait()
        fresh = jnp.dot(normed[...], keyvalue_w[...], preferred_element_type=F32).astype(BF16)
        if pieces > 1:
            fresh = jnp.concatenate([fresh.astype(F32)] * pieces, axis=1)
            fresh = jnp.where(lane // kv_width == me % pieces, fresh, 0.0).astype(BF16)
        fresh_out[t] = fresh
        for j in range(per_group):
            deliver(
                fresh_out.at[t],
                fresh_heads.at[t, fresh_slot],
                send_sem.at[t, 4],
                recv_sem.at[t, 1],
                fresh_group * per_group + j,
            )

        if t == 0:
            @pl.when(section == 0)
            def _():
                for u in range(1, ticks):
                    pltpu.make_async_copy(
                        newcomer_ref.at[u - 1], inputs.at[u, me], recv_sem.at[u, 0]
                    ).start()
                    spread(
                        newcomer_ref.at[u - 1], inputs.at[u, me], send_sem.at[u, 0], recv_sem.at[u, 0]
                    )

        def attend(split):
            owners = n // split
            held = KVH // split
            reach = split * rows * span
            member = lax.rem(me, split)
            cluster = me // split
            keys, values, bias_ref = cache_of(t, split)
            arrived(keys, split, cache_sem.at[t, 0])
            bias = bias_ref[...]
            for i in range(held):
                kv = jnp.where(me >= group_of(member, held // 2, split) * per_group, held - 1 - i, i)
                arrived(heads.at[t], per_group, heads_sem.at[t, kv])
                queries = jnp.concatenate(
                    [heads[t, kv * per_group + j].astype(F32) for j in range(per_group)], axis=0
                ).astype(BF16)
                columns = pl.ds(pl.multiple_of(kv * HD, HD), HD)
                scores = lax.dot_general(
                    queries,
                    keys[:, :, columns].reshape(reach, HD),
                    (((1,), (1,)), ((), ())),
                    preferred_element_type=F32,
                )
                scores = scores.reshape(GROUP, rows, reach) * scale + bias[None]
                top = jnp.maximum(jnp.max(scores, axis=-1, keepdims=True), LEAST)
                weights = jnp.exp(scores - top)
                total = jnp.sum(weights, axis=-1, keepdims=True)
                if i == 0:
                    arrived(values, split, cache_sem.at[t, 1])
                weighted = jnp.dot(
                    weights.reshape(GROUP * rows, reach).astype(BF16),
                    values[:, :, columns].reshape(reach, HD),
                    preferred_element_type=F32,
                )
                for j in range(per_group):
                    these = slice(j * own_heads, (j + 1) * own_heads)
                    stats = packed(top[these], total[these])
                    high = stats.astype(BF16).astype(F32)
                    rest = stats - high
                    middle = rest.astype(BF16).astype(F32)
                    stats = high + pltpu.roll(middle, 1, 1) + pltpu.roll(rest - middle, 2, 1)
                    place = kv * per_group + j
                    staged[t, place] = jnp.concatenate(
                        [weighted[j * own_rows : (j + 1) * own_rows], stats], axis=0
                    ).astype(BF16)
                    deliver(
                        staged.at[t, place],
                        parts.at[t, cluster],
                        send_sem.at[t, 2],
                        recv_sem.at[t, 2],
                        group_of(member, kv, split) * per_group + j,
                    )

        by_section(t, attend)

        arrived(fresh_heads.at[t], 2 * pieces, recv_sem.at[t, 1])
        new_key = jnp.zeros((rows, HD), F32)
        new_value = jnp.zeros((rows, HD), F32)
        for j in range(pieces):
            new_key = new_key + fresh_heads[t, j].astype(F32)
            new_value = new_value + fresh_heads[t, pieces + j].astype(F32)
        new_key = rotated(new_key, t)
        new_score = packed(
            [
                jnp.sum(own_query[h * rows : (h + 1) * rows] * new_key, axis=-1, keepdims=True)
                * scale
                for h in range(own_heads)
            ],
            None,
        )

        def combine(split):
            owners = n // split
            arrived(parts.at[t], owners, recv_sem.at[t, 2])
            sums = []
            blocks = []
            for s in range(owners):
                block = parts[t, s].astype(F32)
                blocks.append(block)
                stats = block[own_rows : own_rows + rows]
                sums.append(stats + pltpu.roll(stats, HD - 1, 1) + pltpu.roll(stats, HD - 2, 1))
            top = new_score
            for s in range(owners):
                top = jnp.maximum(top, sums[s])
            new_weight = jnp.exp(new_score - top)
            denominator = new_weight
            factors = []
            for s in range(owners):
                factors.append(jnp.exp(sums[s] - top))
                denominator = denominator + factors[s] * pltpu.roll(sums[s], HD - 3, 1)
            inverse = 1.0 / denominator
            attended = []
            for h in range(own_heads):
                at = slice(h * stride, h * stride + 1)
                total = (new_weight * inverse)[:, at] * new_value
                for s in range(owners):
                    total = total + (factors[s] * inverse)[:, at] * blocks[s][h * rows : (h + 1) * rows]
                attended.append(total)
            attended = jnp.concatenate(attended, axis=1)
            result = (inputs[t, me].astype(F32) + attended).astype(BF16)
            out_ref[t] = result

        by_section(t, combine)
        if t < ticks - 1 and sections > 1:
            leaving[t] = out_ref[t]

            @pl.when(section < sections - 1)
            def _():
                if t == 0:
                    pl.semaphore_wait(ready_sem, 1)

                def send(step, carry):
                    remote(
                        leaving.at[t],
                        inputs.at[t + 1, me],
                        send_sem.at[t, 3],
                        recv_sem.at[t + 1, 0],
                        section + 1,
                        peer(step, 0),
                    ).start()
                    return carry

                lax.fori_loop(0, n, send, 0)

    for t in range(ticks):
        if t == 0:
            arrived(inputs.at[t], n - 1, send_sem.at[t, 0])
        else:

            @pl.when(section == 0)
            def _():
                arrived(inputs.at[t], n - 1, send_sem.at[t, 0])

        def settle(split):
            owners = n // split
            inside = lax.rem(me, split) == member_of(own_group, split)
            all_sent(heads.at[t], owners, inside, send_sem.at[t, 1])
            all_sent(parts.at[t], owners, inside, send_sem.at[t, 2])
            for kind in range(2):
                arrived(cache_of(t, split)[kind], split - 1, cache_send.at[t, kind])

        by_section(t, settle)
        all_sent(fresh_heads.at[t], per_group, fresh_group == own_group, send_sem.at[t, 4])
        if t < ticks - 1 and sections > 1:

            @pl.when(section < sections - 1)
            def _():
                arrived(inputs.at[t], n, send_sem.at[t, 3])


def shards(
    n,
    sections,
    entering,
    newcomer,
    norm_gain,
    query_weight,
    keyvalue_weight,
    key_cache,
    value_cache,
    cache_lengths,
):
    _, rows, width = entering.shape
    _, features, _ = query_weight.shape
    kv_width = keyvalue_weight.shape[2]
    _, ticks, _, span, kv_features = key_cache.shape
    own_rows = (NH // n) * rows
    pieces = HD // kv_width
    per_group = n // KVH
    chunks = 4
    most = n // NEAR
    later = max(ticks - 1, 1)
    anywhere = pl.BlockSpec(memory_space=pl.ANY)
    out = pl.pallas_call(
        functools.partial(layer_kernel, n, sections),
        out_shape=pltpu.VMEM((ticks, rows, width), BF16),
        in_specs=[anywhere] * 8,
        out_specs=pl.BlockSpec(memory_space=pltpu.VMEM),
        scratch_shapes=[
            pltpu.VMEM((features, width), BF16),
            pltpu.VMEM((features, kv_width), BF16),
            pltpu.VMEM((1, features), BF16),
            pltpu.VMEM((ticks, n, rows, width), BF16),
            pltpu.VMEM((rows, features), BF16),
            pltpu.VMEM((ticks, own_rows, HD), BF16),
            pltpu.VMEM((ticks, most, own_rows, HD), BF16),
            pltpu.VMEM((ticks, rows, HD), BF16),
            pltpu.VMEM((ticks, max(2 * pieces, per_group), rows, HD), BF16),
            pltpu.VMEM((ticks, most, own_rows + rows, HD), BF16),
            pltpu.VMEM((ticks, most, own_rows + rows, HD), BF16),
            pltpu.VMEM((ticks, rows, width), BF16),
            pltpu.SemaphoreType.DMA((3,)),
            pltpu.SemaphoreType.DMA((chunks + 1,)),
            pltpu.SemaphoreType.DMA((ticks, 2)),
            pltpu.SemaphoreType.DMA((ticks, 2)),
            pltpu.SemaphoreType.DMA((ticks, 5)),
            pltpu.SemaphoreType.DMA((ticks, 3)),
            pltpu.SemaphoreType.DMA((ticks, KVH // NEAR)),
            pltpu.SemaphoreType.REGULAR,
            pltpu.VMEM((ticks, rows, NEAR * rows * span), F32),
            pltpu.VMEM((later, rows, WIDE * rows * span), F32),
            pltpu.VMEM((ticks, NEAR, rows * span, kv_features // NEAR), BF16),
            pltpu.VMEM((ticks, NEAR, rows * span, kv_features // NEAR), BF16),
            pltpu.VMEM((later, WIDE, rows * span, kv_features // WIDE), BF16),
            pltpu.VMEM((later, WIDE, rows * span, kv_features // WIDE), BF16),
            pltpu.SMEM(cache_lengths.shape, jnp.int32),
        ],
        compiler_params=pltpu.CompilerParams(
            collective_id=0, has_side_effects=True, vmem_limit_bytes=60 << 20
        ),
    )(
        cache_lengths,
        entering[0],
        newcomer,
        norm_gain,
        query_weight[0],
        keyvalue_weight[0],
        key_cache.reshape(ticks, rows * span, kv_features),
        value_cache.reshape(ticks, rows * span, kv_features),
    )
    return out[None]


def solution(mesh):
    placed = (
        P("section", None, "kvp"),
        P(None, None, "kvp"),
        P("section", None),
        P("section", None, "kvp"),
        P("section", None, "kvp"),
        P("section", None, None, "kvp", None),
        P("section", None, None, "kvp", None),
        P(),
    )
    return jax.shard_map(
        functools.partial(shards, mesh.shape["kvp"], mesh.shape["section"]),
        mesh=mesh,
        in_specs=placed,
        out_specs=P("section", None, None, "kvp"),
        check_vma=False,
    )
```

```python
import functools
import math

import jax
import jax.numpy as jnp
from jax import lax
from jax.experimental import pallas as pl
from jax.experimental.pallas import tpu as pltpu
from jax.sharding import PartitionSpec as P

NH = 64
KVH = 8
HD = 128
GROUP = NH // KVH
THETA = 500000.0
EPS = 1e-05
NEG = -1e30
LEAST = -1e29
MESH = pl.DeviceIdType.MESH
F32 = jnp.float32
BF16 = jnp.bfloat16
NEAR = 2
WIDE = 8


def layer_kernel(
    n,
    sections,
    lengths_hbm,
    entering_ref,
    newcomer_ref,
    gain_hbm,
    query_hbm,
    keyvalue_hbm,
    keys_hbm,
    values_hbm,
    out_ref,
    query_w,
    keyvalue_w,
    gain,
    inputs,
    normed,
    own_heads_out,
    heads,
    fresh_out,
    fresh_heads,
    staged,
    parts,
    leaving,
    load_sem,
    weight_sem,
    cache_sem,
    cache_send,
    send_sem,
    recv_sem,
    heads_sem,
    ready_sem,
    bias_near,
    bias_wide,
    keys_near,
    values_near,
    keys_wide,
    values_wide,
    lengths_ref,
):
    ticks, rows, width = out_ref.shape
    features = query_w.shape[0]
    own_heads = NH // n
    own_rows = own_heads * rows
    kv_width = keyvalue_w.shape[1]
    pieces = HD // kv_width
    per_group = n // KVH
    span = keys_hbm.shape[1] // rows
    chunks = weight_sem.shape[0] - 1
    depth = features // chunks
    scale = 1.0 / math.sqrt(HD)
    stride = HD // own_heads

    section = lax.axis_index("section")
    me = lax.axis_index("kvp")

    own_group = me // per_group

    def peer(step, skip):
        j = jnp.where(me >= n // 2, step, n - 1 - skip - step)
        return j + (j >= me).astype(jnp.int32) if skip else j

    barrier = pltpu.get_barrier_semaphore()

    def greet(step, carry):
        pl.semaphore_signal(
            barrier, inc=1, device_id=(section, peer(step, 1)), device_id_type=MESH
        )
        return carry

    lax.fori_loop(0, n - 1, greet, 0)
    if sections > 1:

        @pl.when(section < sections - 1)
        def _():
            pl.semaphore_signal(barrier, inc=1, device_id=(section + 1, me), device_id_type=MESH)

        @pl.when(section > 0)
        def _():
            pl.semaphore_signal(barrier, inc=1, device_id=(section - 1, me), device_id_type=MESH)

    lengths_load = pltpu.make_async_copy(lengths_hbm, lengths_ref, load_sem.at[2])
    lengths_load.start()
    own_load = pltpu.make_async_copy(entering_ref, inputs.at[0, me], load_sem.at[1])
    own_load.start()
    weight_loads = []
    for c in range(chunks):
        part = pl.ds(c * depth, depth)
        weight_loads.append(
            pltpu.make_async_copy(query_hbm.at[part], query_w.at[part], weight_sem.at[c])
        )
        weight_loads[-1].start()
    gain_load = pltpu.make_async_copy(gain_hbm, gain, load_sem.at[0])
    gain_load.start()
    weight_loads.append(pltpu.make_async_copy(keyvalue_hbm, keyvalue_w, weight_sem.at[chunks]))
    weight_loads[-1].start()

    neighbours = (section > 0).astype(jnp.int32) + (section < sections - 1).astype(jnp.int32)
    pl.semaphore_wait(barrier, n - 1 + neighbours)
    if sections > 1:

        @pl.when(section > 0)
        def _():
            pl.semaphore_signal(ready_sem, inc=1, device_id=(section - 1, me), device_id_type=MESH)

    def remote(source, target, sent, received, to_section, to):
        return pltpu.make_async_remote_copy(
            src_ref=source,
            dst_ref=target,
            send_sem=sent,
            recv_sem=received,
            device_id=(to_section, to),
            device_id_type=MESH,
        )

    def deliver(source, target, sent, received, to):
        @pl.when(to != me)
        def _():
            remote(source, target, sent, received, section, to).start()

        @pl.when(to == me)
        def _():
            pltpu.make_async_copy(source, target, received).start()

    def spread(source, target, sent, received):
        def send(step, carry):
            remote(source, target, sent, received, section, peer(step, 1)).start()
            return carry

        lax.fori_loop(0, n - 1, send, 0)

    def arrived(buffer, count, sem):
        if count:
            whole = buffer.at[pl.ds(0, count)]
            pltpu.make_async_copy(whole, whole, sem).wait()

    def all_sent(buffer, count, at_home, sem):
        @pl.when(at_home)
        def _():
            arrived(buffer, count - 1, sem)

        @pl.when(jnp.logical_not(at_home))
        def _():
            arrived(buffer, count, sem)

    def group_of(member, i, split):
        if split == KVH:
            return member // 2 + lax.rem(member, 2) * (KVH // 2)
        return member * (KVH // split) + i

    def member_of(group, split):
        if split == KVH:
            return lax.rem(group, KVH // 2) * 2 + group // (KVH // 2)
        return group // (KVH // split)

    def owner_slot(group, split):
        return lax.rem(group, KVH // split)

    def cache_of(t, split):
        if split == NEAR:
            return keys_near.at[t], values_near.at[t], bias_near.at[t]
        return keys_wide.at[t - 1], values_wide.at[t - 1], bias_wide.at[t - 1]

    def by_section(t, body):
        if t == 0:
            body(split=NEAR)
        else:
            pl.when(section == 0)(lambda: body(split=NEAR))
            if sections > 1:
                pl.when(section > 0)(lambda: body(split=WIDE))

    def deal_caches(t, split, kinds_now=(0, 1)):
        share = keys_hbm.shape[2] // split
        member = lax.rem(me, split)
        first = me - member
        for kind in kinds_now:
            source = (keys_hbm, values_hbm)[kind]
            target = cache_of(t, split)[kind]
            for i in range(1, split):
                other = lax.rem(member + i, split)
                columns = pl.ds(
                    pl.multiple_of(group_of(other, 0, split) * HD, HD), share
                )
                remote(
                    source.at[t, :, columns],
                    target.at[member],
                    cache_send.at[t, kind],
                    cache_sem.at[t, kind],
                    section,
                    first + other,
                ).start()
            columns = pl.ds(pl.multiple_of(group_of(member, 0, split) * HD, HD), share)
            pltpu.make_async_copy(
                source.at[t, :, columns], target.at[member], cache_sem.at[t, kind]
            ).start()

    spread(entering_ref, inputs.at[0, me], send_sem.at[0, 0], recv_sem.at[0, 0])
    for t in range(ticks):
        by_section(t, functools.partial(deal_caches, t, kinds_now=(0, 1) if t == 0 else (0,)))

    lane = lax.broadcasted_iota(jnp.int32, (rows, HD), 1)
    half = HD // 2
    exponent = (lane % half).astype(F32) * (2.0 / HD)
    frequency = jnp.exp(exponent * (-math.log(THETA)))
    lengths_load.wait()

    def lengths_of(t, shape):
        request = lax.broadcasted_iota(jnp.int32, shape, 0)
        lengths = jnp.zeros(shape, jnp.int32)
        for b in range(rows):
            length = lengths_ref[t + sections - 1 - section, b]
            lengths = jnp.where(request == b, length, lengths)
        return request, lengths

    def put_bias(t, split):
        shape = (rows, split * rows * span)
        request, limit = lengths_of(t, shape)
        place = lax.broadcasted_iota(jnp.int32, shape, 1)
        slot = place // (rows * span)
        position = (me // split * split + slot) * span + place % span
        valid = (place // span % rows == request) & (position < limit)
        cache_of(t, split)[2][...] = jnp.where(valid, 0.0, NEG).astype(F32)

    turns = []
    for t in range(ticks):
        angles = lengths_of(t, (rows, HD))[1].astype(F32) * frequency
        sine = jnp.sin(angles)
        turns.append((jnp.cos(angles), jnp.where(lane < half, -sine, sine)))
        by_section(t, functools.partial(put_bias, t))

    def rotated(head, t):
        cosine, sine = turns[t]
        return head * cosine + pltpu.roll(head, half, 1) * sine

    def packed(tops, totals):
        p = jnp.zeros((rows, HD), F32)
        for h in range(own_heads):
            p = jnp.where(lane == h * stride, tops[h], p)
            if totals is not None:
                p = jnp.where(lane == h * stride + 3, totals[h], p)
        return p

    kinds = n // 2
    fresh_group = (me % kinds) // pieces
    fresh_slot = (me // kinds) * pieces + me % pieces

    gain_load.wait()
    for t in range(ticks):
        if t == 0:
            own_load.wait()
            arrived(inputs.at[0], n - 1, recv_sem.at[0, 0])
        else:
            arrived(inputs.at[t], n, recv_sem.at[t, 0])

        squares = jnp.zeros((rows, width), F32)
        for s in range(n):
            x = inputs[t, s].astype(F32)
            squares = squares + x * x
        mean_square = jnp.sum(squares, axis=-1, keepdims=True) * (1.0 / features)
        factor = lax.rsqrt(mean_square + EPS)
        for s in range(n):
            part = pl.ds(s * width, width)
            x = inputs[t, s].astype(F32)
            normed[:, part] = (x * factor * gain[:, part].astype(F32)).astype(BF16)

        query = jnp.zeros((rows, width), F32)
        for c in range(chunks):
            part = pl.ds(c * depth, depth)
            if t == 0:
                weight_loads[c].wait()
            query = query + jnp.dot(normed[:, part], query_w[part], preferred_element_type=F32)
        own_query = jnp.concatenate(
            [rotated(query[:, h * HD : (h + 1) * HD], t) for h in range(own_heads)], axis=0
        ).astype(BF16)
        own_heads_out[t] = own_query
        own_query = own_query.astype(F32)
        def send_heads(split):
            owners = n // split
            cluster = me // split
            home = member_of(own_group, split)
            slot = owner_slot(own_group, split) * per_group + lax.rem(me, per_group)

            def send(step, carry):
                to = jnp.where(cluster >= owners // 2, step, owners - 1 - step) * split + home
                deliver(
                    own_heads_out.at[t],
                    heads.at[t, slot],
                    send_sem.at[t, 1],
                    heads_sem.at[t, slot // per_group],
                    to,
                )
                return carry

            lax.fori_loop(0, owners, send, 0)

        by_section(t, send_heads)
        if t == 0:
            for u in range(1, ticks):
                by_section(u, functools.partial(deal_caches, u, kinds_now=(1,)))

        if t == 0:
            weight_loads[chunks].wait()
        fresh = jnp.dot(normed[...], keyvalue_w[...], preferred_element_type=F32).astype(BF16)
        if pieces > 1:
            fresh = jnp.concatenate([fresh.astype(F32)] * pieces, axis=1)
            fresh = jnp.where(lane // kv_width == me % pieces, fresh, 0.0).astype(BF16)
        fresh_out[t] = fresh
        for j in range(per_group):
            deliver(
                fresh_out.at[t],
                fresh_heads.at[t, fresh_slot],
                send_sem.at[t, 4],
                recv_sem.at[t, 1],
                fresh_group * per_group + j,
            )

        if t == 0:
            @pl.when(section == 0)
            def _():
                for u in range(1, ticks):
                    pltpu.make_async_copy(
                        newcomer_ref.at[u - 1], inputs.at[u, me], recv_sem.at[u, 0]
                    ).start()
                    spread(
                        newcomer_ref.at[u - 1], inputs.at[u, me], send_sem.at[u, 0], recv_sem.at[u, 0]
                    )

        def attend(split):
            owners = n // split
            held = KVH // split
            reach = split * rows * span
            member = lax.rem(me, split)
            cluster = me // split
            keys, values, bias_ref = cache_of(t, split)
            arrived(keys, split, cache_sem.at[t, 0])
            bias = bias_ref[...]
            for i in range(held):
                kv = jnp.where(me >= group_of(member, held // 2, split) * per_group, held - 1 - i, i)
                arrived(heads.at[t], per_group, heads_sem.at[t, kv])
                queries = jnp.concatenate(
                    [heads[t, kv * per_group + j].astype(F32) for j in range(per_group)], axis=0
                ).astype(BF16)
                columns = pl.ds(pl.multiple_of(kv * HD, HD), HD)
                scores = lax.dot_general(
                    queries,
                    keys[:, :, columns].reshape(reach, HD),
                    (((1,), (1,)), ((), ())),
                    preferred_element_type=F32,
                )
                scores = scores.reshape(GROUP, rows, reach) * scale + bias[None]
                top = jnp.maximum(jnp.max(scores, axis=-1, keepdims=True), LEAST)
                weights = jnp.exp(scores - top)
                total = jnp.sum(weights, axis=-1, keepdims=True)
                if i == 0:
                    arrived(values, split, cache_sem.at[t, 1])
                weighted = jnp.dot(
                    weights.reshape(GROUP * rows, reach).astype(BF16),
                    values[:, :, columns].reshape(reach, HD),
                    preferred_element_type=F32,
                )
                for j in range(per_group):
                    these = slice(j * own_heads, (j + 1) * own_heads)
                    stats = packed(top[these], total[these])
                    high = stats.astype(BF16).astype(F32)
                    rest = stats - high
                    middle = rest.astype(BF16).astype(F32)
                    stats = high + pltpu.roll(middle, 1, 1) + pltpu.roll(rest - middle, 2, 1)
                    place = kv * per_group + j
                    staged[t, place] = jnp.concatenate(
                        [weighted[j * own_rows : (j + 1) * own_rows], stats], axis=0
                    ).astype(BF16)
                    deliver(
                        staged.at[t, place],
                        parts.at[t, cluster],
                        send_sem.at[t, 2],
                        recv_sem.at[t, 2],
                        group_of(member, kv, split) * per_group + j,
                    )

        by_section(t, attend)

        arrived(fresh_heads.at[t], 2 * pieces, recv_sem.at[t, 1])
        new_key = jnp.zeros((rows, HD), F32)
        new_value = jnp.zeros((rows, HD), F32)
        for j in range(pieces):
            new_key = new_key + fresh_heads[t, j].astype(F32)
            new_value = new_value + fresh_heads[t, pieces + j].astype(F32)
        new_key = rotated(new_key, t)
        new_score = packed(
            [
                jnp.sum(own_query[h * rows : (h + 1) * rows] * new_key, axis=-1, keepdims=True)
                * scale
                for h in range(own_heads)
            ],
            None,
        )

        def combine(split):
            owners = n // split
            arrived(parts.at[t], owners, recv_sem.at[t, 2])
            sums = []
            blocks = []
            for s in range(owners):
                block = parts[t, s].astype(F32)
                blocks.append(block)
                stats = block[own_rows : own_rows + rows]
                sums.append(stats + pltpu.roll(stats, HD - 1, 1) + pltpu.roll(stats, HD - 2, 1))
            top = new_score
            for s in range(owners):
                top = jnp.maximum(top, sums[s])
            new_weight = jnp.exp(new_score - top)
            denominator = new_weight
            factors = []
            for s in range(owners):
                factors.append(jnp.exp(sums[s] - top))
                denominator = denominator + factors[s] * pltpu.roll(sums[s], HD - 3, 1)
            inverse = 1.0 / denominator
            attended = []
            for h in range(own_heads):
                at = slice(h * stride, h * stride + 1)
                total = (new_weight * inverse)[:, at] * new_value
                for s in range(owners):
                    total = total + (factors[s] * inverse)[:, at] * blocks[s][h * rows : (h + 1) * rows]
                attended.append(total)
            attended = jnp.concatenate(attended, axis=1)
            result = (inputs[t, me].astype(F32) + attended).astype(BF16)
            out_ref[t] = result

        by_section(t, combine)
        if t < ticks - 1 and sections > 1:
            leaving[t] = out_ref[t]

            @pl.when(section < sections - 1)
            def _():
                if t == 0:
                    pl.semaphore_wait(ready_sem, 1)

                def send(step, carry):
                    remote(
                        leaving.at[t],
                        inputs.at[t + 1, me],
                        send_sem.at[t, 3],
                        recv_sem.at[t + 1, 0],
                        section + 1,
                        peer(step, 0),
                    ).start()
                    return carry

                lax.fori_loop(0, n, send, 0)

    for t in range(ticks):
        if t == 0:
            arrived(inputs.at[t], n - 1, send_sem.at[t, 0])
        else:

            @pl.when(section == 0)
            def _():
                arrived(inputs.at[t], n - 1, send_sem.at[t, 0])

        def settle(split):
            owners = n // split
            inside = lax.rem(me, split) == member_of(own_group, split)
            all_sent(heads.at[t], owners, inside, send_sem.at[t, 1])
            all_sent(parts.at[t], owners, inside, send_sem.at[t, 2])
            for kind in range(2):
                arrived(cache_of(t, split)[kind], split - 1, cache_send.at[t, kind])

        by_section(t, settle)
        all_sent(fresh_heads.at[t], per_group, fresh_group == own_group, send_sem.at[t, 4])
        if t < ticks - 1 and sections > 1:

            @pl.when(section < sections - 1)
            def _():
                arrived(inputs.at[t], n, send_sem.at[t, 3])


def shards(
    n,
    sections,
    entering,
    newcomer,
    norm_gain,
    query_weight,
    keyvalue_weight,
    key_cache,
    value_cache,
    cache_lengths,
):
    _, rows, width = entering.shape
    _, features, _ = query_weight.shape
    kv_width = keyvalue_weight.shape[2]
    _, ticks, _, span, kv_features = key_cache.shape
    own_rows = (NH // n) * rows
    pieces = HD // kv_width
    per_group = n // KVH
    chunks = 4
    most = n // NEAR
    later = max(ticks - 1, 1)
    anywhere = pl.BlockSpec(memory_space=pl.ANY)
    out = pl.pallas_call(
        functools.partial(layer_kernel, n, sections),
        out_shape=pltpu.VMEM((ticks, rows, width), BF16),
        in_specs=[anywhere] * 8,
        out_specs=pl.BlockSpec(memory_space=pltpu.VMEM),
        scratch_shapes=[
            pltpu.VMEM((features, width), BF16),
            pltpu.VMEM((features, kv_width), BF16),
            pltpu.VMEM((1, features), BF16),
            pltpu.VMEM((ticks, n, rows, width), BF16),
            pltpu.VMEM((rows, features), BF16),
            pltpu.VMEM((ticks, own_rows, HD), BF16),
            pltpu.VMEM((ticks, most, own_rows, HD), BF16),
            pltpu.VMEM((ticks, rows, HD), BF16),
            pltpu.VMEM((ticks, max(2 * pieces, per_group), rows, HD), BF16),
            pltpu.VMEM((ticks, most, own_rows + rows, HD), BF16),
            pltpu.VMEM((ticks, most, own_rows + rows, HD), BF16),
            pltpu.VMEM((ticks, rows, width), BF16),
            pltpu.SemaphoreType.DMA((3,)),
            pltpu.SemaphoreType.DMA((chunks + 1,)),
            pltpu.SemaphoreType.DMA((ticks, 2)),
            pltpu.SemaphoreType.DMA((ticks, 2)),
            pltpu.SemaphoreType.DMA((ticks, 5)),
            pltpu.SemaphoreType.DMA((ticks, 3)),
            pltpu.SemaphoreType.DMA((ticks, KVH // NEAR)),
            pltpu.SemaphoreType.REGULAR,
            pltpu.VMEM((ticks, rows, NEAR * rows * span), F32),
            pltpu.VMEM((later, rows, WIDE * rows * span), F32),
            pltpu.VMEM((ticks, NEAR, rows * span, kv_features // NEAR), BF16),
            pltpu.VMEM((ticks, NEAR, rows * span, kv_features // NEAR), BF16),
            pltpu.VMEM((later, WIDE, rows * span, kv_features // WIDE), BF16),
            pltpu.VMEM((later, WIDE, rows * span, kv_features // WIDE), BF16),
            pltpu.SMEM(cache_lengths.shape, jnp.int32),
        ],
        compiler_params=pltpu.CompilerParams(
            collective_id=0, has_side_effects=True, vmem_limit_bytes=60 << 20
        ),
    )(
        cache_lengths,
        entering[0],
        newcomer,
        norm_gain,
        query_weight[0],
        keyvalue_weight[0],
        key_cache.reshape(ticks, rows * span, kv_features),
        value_cache.reshape(ticks, rows * span, kv_features),
    )
    return out[None]


def solution(mesh):
    placed = (
        P("section", None, "kvp"),
        P(None, None, "kvp"),
        P("section", None),
        P("section", None, "kvp"),
        P("section", None, "kvp"),
        P("section", None, None, "kvp", None),
        P("section", None, None, "kvp", None),
        P(),
    )
    return jax.shard_map(
        functools.partial(shards, mesh.shape["kvp"], mesh.shape["section"]),
        mesh=mesh,
        in_specs=placed,
        out_specs=P("section", None, None, "kvp"),
        check_vma=False,
    )
```

```python
import functools
import math

import jax
import jax.numpy as jnp
from jax import lax
from jax.experimental import pallas as pl
from jax.experimental.pallas import tpu as pltpu
from jax.sharding import PartitionSpec as P

NH = 64
KVH = 8
HD = 128
GROUP = NH // KVH
THETA = 500000.0
EPS = 1e-05
NEG = -1e30
LEAST = -1e29
MESH = pl.DeviceIdType.MESH
F32 = jnp.float32
BF16 = jnp.bfloat16
NEAR = 2
WIDE = 8
TOGETHER = 2


def layer_kernel(
    n,
    sections,
    lengths_hbm,
    entering_ref,
    newcomer_ref,
    gain_hbm,
    query_hbm,
    keyvalue_hbm,
    keys_hbm,
    values_hbm,
    out_ref,
    query_w,
    keyvalue_w,
    gain,
    inputs,
    normed,
    own_heads_out,
    heads,
    fresh_out,
    fresh_heads,
    staged,
    parts,
    leaving,
    load_sem,
    weight_sem,
    cache_sem,
    cache_send,
    send_sem,
    recv_sem,
    heads_sem,
    ready_sem,
    bias_near,
    bias_wide,
    keys_near,
    values_near,
    keys_wide,
    values_wide,
    lengths_ref,
):
    ticks, rows, width = out_ref.shape
    features = query_w.shape[0]
    own_heads = NH // n
    own_rows = own_heads * rows
    kv_width = keyvalue_w.shape[1]
    pieces = HD // kv_width
    per_group = n // KVH
    span = keys_hbm.shape[1] // rows
    chunks = weight_sem.shape[0] - 1
    depth = features // chunks
    scale = 1.0 / math.sqrt(HD)
    stride = HD // own_heads

    section = lax.axis_index("section")
    me = lax.axis_index("kvp")

    own_group = me // per_group

    def peer(step, skip):
        j = jnp.where(me >= n // 2, step, n - 1 - skip - step)
        return j + (j >= me).astype(jnp.int32) if skip else j

    barrier = pltpu.get_barrier_semaphore()

    def greet(step, carry):
        pl.semaphore_signal(
            barrier, inc=1, device_id=(section, peer(step, 1)), device_id_type=MESH
        )
        return carry

    lax.fori_loop(0, n - 1, greet, 0)
    if sections > 1:

        @pl.when(section < sections - 1)
        def _():
            pl.semaphore_signal(barrier, inc=1, device_id=(section + 1, me), device_id_type=MESH)

        @pl.when(section > 0)
        def _():
            pl.semaphore_signal(barrier, inc=1, device_id=(section - 1, me), device_id_type=MESH)

    lengths_load = pltpu.make_async_copy(lengths_hbm, lengths_ref, load_sem.at[2])
    lengths_load.start()
    own_load = pltpu.make_async_copy(entering_ref, inputs.at[0, me], load_sem.at[1])
    own_load.start()
    weight_loads = []
    for c in range(chunks):
        part = pl.ds(c * depth, depth)
        weight_loads.append(
            pltpu.make_async_copy(query_hbm.at[part], query_w.at[part], weight_sem.at[c])
        )
        weight_loads[-1].start()
    gain_load = pltpu.make_async_copy(gain_hbm, gain, load_sem.at[0])
    gain_load.start()
    weight_loads.append(pltpu.make_async_copy(keyvalue_hbm, keyvalue_w, weight_sem.at[chunks]))
    weight_loads[-1].start()

    neighbours = (section > 0).astype(jnp.int32) + (section < sections - 1).astype(jnp.int32)
    pl.semaphore_wait(barrier, n - 1 + neighbours)
    if sections > 1:

        @pl.when(section > 0)
        def _():
            pl.semaphore_signal(ready_sem, inc=1, device_id=(section - 1, me), device_id_type=MESH)

    def remote(source, target, sent, received, to_section, to):
        return pltpu.make_async_remote_copy(
            src_ref=source,
            dst_ref=target,
            send_sem=sent,
            recv_sem=received,
            device_id=(to_section, to),
            device_id_type=MESH,
        )

    def deliver(source, target, sent, received, to):
        @pl.when(to != me)
        def _():
            remote(source, target, sent, received, section, to).start()

        @pl.when(to == me)
        def _():
            pltpu.make_async_copy(source, target, received).start()

    def spread(source, target, sent, received):
        def send(step, carry):
            remote(source, target, sent, received, section, peer(step, 1)).start()
            return carry

        lax.fori_loop(0, n - 1, send, 0)

    def arrived(buffer, count, sem):
        if count:
            whole = buffer.at[pl.ds(0, count)]
            pltpu.make_async_copy(whole, whole, sem).wait()

    def all_sent(buffer, count, at_home, sem):
        @pl.when(at_home)
        def _():
            arrived(buffer, count - 1, sem)

        @pl.when(jnp.logical_not(at_home))
        def _():
            arrived(buffer, count, sem)

    def crossed(i):
        return i // 4 * 4 + lax.rem(i, 2) * 2 + lax.rem(i // 2, 2)

    def group_of(member, i, split):
        return crossed(member) if split == KVH else member * (KVH // split) + i

    def member_of(group, split):
        return crossed(group) if split == KVH else group // (KVH // split)

    def owner_slot(group, split):
        return lax.rem(group, KVH // split)

    def cache_of(t, split):
        if split == NEAR:
            return keys_near.at[t], values_near.at[t], bias_near.at[t]
        return keys_wide.at[t - 1], values_wide.at[t - 1], bias_wide.at[t - 1]

    def by_section(t, body):
        if t == 0:
            body(split=NEAR)
        else:
            pl.when(section == 0)(lambda: body(split=NEAR))
            if sections > 1:
                pl.when(section > 0)(lambda: body(split=WIDE))

    def deal_caches(t, split, kinds_now=(0, 1)):
        share = keys_hbm.shape[2] // split
        member = lax.rem(me, split)
        first = me - member
        for kind in kinds_now:
            source = (keys_hbm, values_hbm)[kind]
            target = cache_of(t, split)[kind]
            for i in range(1, split):
                other = lax.rem(member + i, split)
                columns = pl.ds(
                    pl.multiple_of(group_of(other, 0, split) * HD, HD), share
                )
                remote(
                    source.at[t, :, columns],
                    target.at[member],
                    cache_send.at[t, kind],
                    cache_sem.at[t, kind],
                    section,
                    first + other,
                ).start()
            columns = pl.ds(pl.multiple_of(group_of(member, 0, split) * HD, HD), share)
            pltpu.make_async_copy(
                source.at[t, :, columns], target.at[member], cache_sem.at[t, kind]
            ).start()

    spread(entering_ref, inputs.at[0, me], send_sem.at[0, 0], recv_sem.at[0, 0])

    @pl.when(section == 0)
    def _():
        for t in range(1, ticks):
            target = inputs.at[t, me]
            pltpu.make_async_copy(newcomer_ref.at[t - 1], target, recv_sem.at[t, 0]).start()
            spread(newcomer_ref.at[t - 1], target, send_sem.at[t, 0], recv_sem.at[t, 0])

    for t in range(ticks):
        by_section(t, functools.partial(deal_caches, t, kinds_now=(0, 1) if t == 0 else (0,)))

    lane = lax.broadcasted_iota(jnp.int32, (rows, HD), 1)
    half = HD // 2
    exponent = (lane % half).astype(F32) * (2.0 / HD)
    frequency = jnp.exp(exponent * (-math.log(THETA)))
    lengths_load.wait()

    def lengths_of(t, shape):
        request = lax.broadcasted_iota(jnp.int32, shape, 0)
        lengths = jnp.zeros(shape, jnp.int32)
        for b in range(rows):
            length = lengths_ref[t + sections - 1 - section, b]
            lengths = jnp.where(request == b, length, lengths)
        return request, lengths

    def put_bias(t, split):
        block, chunk = split * span, cache_of(t, split)[2].shape[1]
        request, limit = lengths_of(t, (rows, chunk))
        place = lax.broadcasted_iota(jnp.int32, (rows, chunk), 1)
        slot = place % block // span
        position = (me // split * split + slot) * span + place % span
        valid = (place // block == request % (chunk // block)) & (position < limit)
        cache_of(t, split)[2][...] = jnp.where(valid, 0.0, NEG).astype(F32)

    turns = []
    for t in range(ticks):
        angles = lengths_of(t, (rows, HD))[1].astype(F32) * frequency
        sine = jnp.sin(angles)
        turns.append((jnp.cos(angles), jnp.where(lane < half, -sine, sine)))
        by_section(t, functools.partial(put_bias, t))

    def rotated(head, t):
        cosine, sine = turns[t]
        return head * cosine + pltpu.roll(head, half, 1) * sine

    def packed(tops, totals):
        p = jnp.zeros((rows, HD), F32)
        for h in range(own_heads):
            p = jnp.where(lane == h * stride, tops[h], p)
            if totals is not None:
                p = jnp.where(lane == h * stride + 3, totals[h], p)
        return p

    kinds = n // 2
    fresh_group = (me % kinds) // pieces
    fresh_slot = (me // kinds) * pieces + me % pieces

    def find_query(t):
        if t == 0:
            own_load.wait()
            arrived(inputs.at[0], n - 1, recv_sem.at[0, 0])
        else:
            arrived(inputs.at[t], n, recv_sem.at[t, 0])

        squares = jnp.zeros((rows, width), F32)
        for s in range(n):
            x = inputs[t, s].astype(F32)
            squares = squares + x * x
        mean_square = jnp.sum(squares, axis=-1, keepdims=True) * (1.0 / features)
        factor = lax.rsqrt(mean_square + EPS)
        for s in range(n):
            part = pl.ds(s * width, width)
            x = inputs[t, s].astype(F32)
            normed[:, part] = (x * factor * gain[:, part].astype(F32)).astype(BF16)

        query = jnp.zeros((rows, width), F32)
        for c in range(chunks):
            part = pl.ds(c * depth, depth)
            if t == 0:
                weight_loads[c].wait()
            query = query + jnp.dot(normed[:, part], query_w[part], preferred_element_type=F32)
        own_query = jnp.concatenate(
            [rotated(query[:, h * HD : (h + 1) * HD], t) for h in range(own_heads)], axis=0
        ).astype(BF16)
        own_heads_out[t] = own_query

    def send_query(t, split):
        owners = n // split
        cluster = me // split
        home = member_of(own_group, split)
        slot = owner_slot(own_group, split) * per_group + lax.rem(me, per_group)

        def send(step, carry):
            to = jnp.where(cluster >= owners // 2, step, owners - 1 - step) * split + home
            deliver(
                own_heads_out.at[t],
                heads.at[t, slot],
                send_sem.at[t, 1],
                heads_sem.at[t, slot // per_group],
                to,
            )
            return carry

        lax.fori_loop(0, owners, send, 0)

    def find_fresh(t):
        if t == 0:
            weight_loads[chunks].wait()
        fresh = jnp.dot(normed[...], keyvalue_w[...], preferred_element_type=F32).astype(BF16)
        if pieces > 1:
            fresh = jnp.concatenate([fresh.astype(F32)] * pieces, axis=1)
            fresh = jnp.where(lane // kv_width == me % pieces, fresh, 0.0).astype(BF16)
        fresh_out[t] = fresh

    def send_fresh(t):
        for j in range(per_group):
            deliver(
                fresh_out.at[t],
                fresh_heads.at[t, fresh_slot],
                send_sem.at[t, 4],
                recv_sem.at[t, 1],
                fresh_group * per_group + j,
            )

    gain_load.wait()
    find_query(0)
    send_query(0, NEAR)
    for t in range(1, ticks):
        by_section(t, functools.partial(deal_caches, t, kinds_now=(1,)))
    find_fresh(0)
    send_fresh(0)

    @pl.when(section == 0)
    def _():
        for t in range(1, ticks):
            find_query(t)
            send_query(t, NEAR)
            find_fresh(t)
            send_fresh(t)

    for t in range(ticks):
        def attend(split):
            owners = n // split
            held = KVH // split
            member = lax.rem(me, split)
            cluster = me // split
            keys, values, bias_ref = cache_of(t, split)
            arrived(keys, split, cache_sem.at[t, 0])
            bias = bias_ref[...]
            block, chunk = split * span, bias.shape[1]
            per = chunk // block
            request = lax.broadcasted_iota(jnp.int32, (rows, chunk), 0)

            def chunk_of(cache, v, columns):
                return jnp.concatenate(
                    [
                        cache[:, b * span : (b + 1) * span, columns].reshape(block, HD)
                        for b in range(v * per, (v + 1) * per)
                    ],
                    axis=0,
                )

            def one_head(kv):
                queries = jnp.concatenate(
                    [heads[t, kv * per_group + j].astype(F32) for j in range(per_group)], axis=0
                ).astype(BF16)
                columns = pl.ds(pl.multiple_of(kv * HD, HD), HD)
                scores = None
                for v in range(rows // per):
                    part = lax.dot_general(
                        queries,
                        chunk_of(keys, v, columns),
                        (((1,), (1,)), ((), ())),
                        preferred_element_type=F32,
                    ).reshape(GROUP, rows, chunk)
                    scores = part if v == 0 else jnp.where(request // per == v, part, scores)
                scores = scores * scale + bias
                top = jnp.maximum(jnp.max(scores, axis=-1, keepdims=True), LEAST)
                weights = jnp.exp(scores - top)
                total = jnp.sum(weights, axis=-1, keepdims=True)
                weighted = jnp.zeros((GROUP * rows, HD), F32)
                for v in range(rows // per):
                    weighted = weighted + jnp.dot(
                        jnp.where(request // per == v, weights, 0.0)
                        .reshape(GROUP * rows, chunk)
                        .astype(BF16),
                        chunk_of(values, v, columns),
                        preferred_element_type=F32,
                    )
                return top, total, weighted

            arrived(values, split, cache_sem.at[t, 1])
            ordered = [
                jnp.where(me >= group_of(member, held // 2, split) * per_group, held - 1 - i, i)
                for i in range(held)
            ]
            for i in range(0, held, TOGETHER):
                some = ordered[i : i + TOGETHER]
                for kv in some:
                    arrived(heads.at[t], per_group, heads_sem.at[t, kv])
                found = [one_head(kv) for kv in some]
                for kv, (top, total, weighted) in zip(some, found):
                    for j in range(per_group):
                        these = slice(j * own_heads, (j + 1) * own_heads)
                        stats = packed(top[these], total[these])
                        high = stats.astype(BF16).astype(F32)
                        rest = stats - high
                        middle = rest.astype(BF16).astype(F32)
                        stats = high + pltpu.roll(middle, 1, 1) + pltpu.roll(rest - middle, 2, 1)
                        place = kv * per_group + j
                        staged[t, place] = jnp.concatenate(
                            [weighted[j * own_rows : (j + 1) * own_rows], stats], axis=0
                        ).astype(BF16)
                        deliver(
                            staged.at[t, place],
                            parts.at[t, cluster],
                            send_sem.at[t, 2],
                            recv_sem.at[t, 2],
                            group_of(member, kv, split) * per_group + j,
                        )

        by_section(t, attend)

        arrived(fresh_heads.at[t], 2 * pieces, recv_sem.at[t, 1])
        own_query = own_heads_out[t].astype(F32)
        new_key = jnp.zeros((rows, HD), F32)
        new_value = jnp.zeros((rows, HD), F32)
        for j in range(pieces):
            new_key = new_key + fresh_heads[t, j].astype(F32)
            new_value = new_value + fresh_heads[t, pieces + j].astype(F32)
        new_key = rotated(new_key, t)
        new_score = packed(
            [
                jnp.sum(own_query[h * rows : (h + 1) * rows] * new_key, axis=-1, keepdims=True)
                * scale
                for h in range(own_heads)
            ],
            None,
        )

        def combine(split):
            owners = n // split
            arrived(parts.at[t], owners, recv_sem.at[t, 2])
            sums = []
            blocks = []
            for s in range(owners):
                block = parts[t, s].astype(F32)
                blocks.append(block)
                stats = block[own_rows : own_rows + rows]
                sums.append(stats + pltpu.roll(stats, HD - 1, 1) + pltpu.roll(stats, HD - 2, 1))
            top = new_score
            for s in range(owners):
                top = jnp.maximum(top, sums[s])
            new_weight = jnp.exp(new_score - top)
            denominator = new_weight
            factors = []
            for s in range(owners):
                factors.append(jnp.exp(sums[s] - top))
                denominator = denominator + factors[s] * pltpu.roll(sums[s], HD - 3, 1)
            inverse = 1.0 / denominator
            attended = []
            for h in range(own_heads):
                at = slice(h * stride, h * stride + 1)
                total = (new_weight * inverse)[:, at] * new_value
                for s in range(owners):
                    total = total + (factors[s] * inverse)[:, at] * blocks[s][h * rows : (h + 1) * rows]
                attended.append(total)
            attended = jnp.concatenate(attended, axis=1)
            result = (inputs[t, me].astype(F32) + attended).astype(BF16)
            out_ref[t] = result

        by_section(t, combine)
        if t < ticks - 1 and sections > 1:
            leaving[t] = out_ref[t]

            @pl.when(section < sections - 1)
            def _():
                if t == 0:
                    pl.semaphore_wait(ready_sem, 1)

                def send(step, carry):
                    remote(
                        leaving.at[t],
                        inputs.at[t + 1, me],
                        send_sem.at[t, 3],
                        recv_sem.at[t + 1, 0],
                        section + 1,
                        peer(step, 0),
                    ).start()
                    return carry

                lax.fori_loop(0, n, send, 0)

        if t < ticks - 1 and sections > 1:

            @pl.when(section > 0)
            def _():
                find_query(t + 1)
                send_query(t + 1, WIDE)
                find_fresh(t + 1)
                send_fresh(t + 1)

    for t in range(ticks):
        if t == 0:
            arrived(inputs.at[t], n - 1, send_sem.at[t, 0])
        else:

            @pl.when(section == 0)
            def _():
                arrived(inputs.at[t], n - 1, send_sem.at[t, 0])

        def settle(split):
            owners = n // split
            inside = lax.rem(me, split) == member_of(own_group, split)
            all_sent(heads.at[t], owners, inside, send_sem.at[t, 1])
            all_sent(parts.at[t], owners, inside, send_sem.at[t, 2])
            for kind in range(2):
                arrived(cache_of(t, split)[kind], split - 1, cache_send.at[t, kind])

        by_section(t, settle)
        all_sent(fresh_heads.at[t], per_group, fresh_group == own_group, send_sem.at[t, 4])
        if t < ticks - 1 and sections > 1:

            @pl.when(section < sections - 1)
            def _():
                arrived(inputs.at[t], n, send_sem.at[t, 3])


def shards(
    n,
    sections,
    entering,
    newcomer,
    norm_gain,
    query_weight,
    keyvalue_weight,
    key_cache,
    value_cache,
    cache_lengths,
):
    _, rows, width = entering.shape
    _, features, _ = query_weight.shape
    kv_width = keyvalue_weight.shape[2]
    _, ticks, _, span, kv_features = key_cache.shape
    own_rows = (NH // n) * rows
    pieces = HD // kv_width
    per_group = n // KVH
    chunks = 4
    most = n // NEAR
    later = max(ticks - 1, 1)
    anywhere = pl.BlockSpec(memory_space=pl.ANY)
    out = pl.pallas_call(
        functools.partial(layer_kernel, n, sections),
        out_shape=pltpu.VMEM((ticks, rows, width), BF16),
        in_specs=[anywhere] * 8,
        out_specs=pl.BlockSpec(memory_space=pltpu.VMEM),
        scratch_shapes=[
            pltpu.VMEM((features, width), BF16),
            pltpu.VMEM((features, kv_width), BF16),
            pltpu.VMEM((1, features), BF16),
            pltpu.VMEM((ticks, n, rows, width), BF16),
            pltpu.VMEM((rows, features), BF16),
            pltpu.VMEM((ticks, own_rows, HD), BF16),
            pltpu.VMEM((ticks, most, own_rows, HD), BF16),
            pltpu.VMEM((ticks, rows, HD), BF16),
            pltpu.VMEM((ticks, max(2 * pieces, per_group), rows, HD), BF16),
            pltpu.VMEM((ticks, most, own_rows + rows, HD), BF16),
            pltpu.VMEM((ticks, most, own_rows + rows, HD), BF16),
            pltpu.VMEM((ticks, rows, width), BF16),
            pltpu.SemaphoreType.DMA((3,)),
            pltpu.SemaphoreType.DMA((chunks + 1,)),
            pltpu.SemaphoreType.DMA((ticks, 2)),
            pltpu.SemaphoreType.DMA((ticks, 2)),
            pltpu.SemaphoreType.DMA((ticks, 5)),
            pltpu.SemaphoreType.DMA((ticks, 3)),
            pltpu.SemaphoreType.DMA((ticks, KVH // NEAR)),
            pltpu.SemaphoreType.REGULAR,
            pltpu.VMEM((ticks, rows, max(NEAR * span, HD)), F32),
            pltpu.VMEM((later, rows, max(WIDE * span, HD)), F32),
            pltpu.VMEM((ticks, NEAR, rows * span, kv_features // NEAR), BF16),
            pltpu.VMEM((ticks, NEAR, rows * span, kv_features // NEAR), BF16),
            pltpu.VMEM((later, WIDE, rows * span, kv_features // WIDE), BF16),
            pltpu.VMEM((later, WIDE, rows * span, kv_features // WIDE), BF16),
            pltpu.SMEM(cache_lengths.shape, jnp.int32),
        ],
        compiler_params=pltpu.CompilerParams(
            collective_id=0, has_side_effects=True, vmem_limit_bytes=60 << 20
        ),
    )(
        cache_lengths,
        entering[0],
        newcomer,
        norm_gain,
        query_weight[0],
        keyvalue_weight[0],
        key_cache.reshape(ticks, rows * span, kv_features),
        value_cache.reshape(ticks, rows * span, kv_features),
    )
    return out[None]


def solution(mesh):
    placed = (
        P("section", None, "kvp"),
        P(None, None, "kvp"),
        P("section", None),
        P("section", None, "kvp"),
        P("section", None, "kvp"),
        P("section", None, None, "kvp", None),
        P("section", None, None, "kvp", None),
        P(),
    )
    return jax.shard_map(
        functools.partial(shards, mesh.shape["kvp"], mesh.shape["section"]),
        mesh=mesh,
        in_specs=placed,
        out_specs=P("section", None, None, "kvp"),
        check_vma=False,
    )
```

```python
import functools
import math

import jax
import jax.numpy as jnp
from jax import lax
from jax.experimental import pallas as pl
from jax.experimental.pallas import tpu as pltpu
from jax.sharding import PartitionSpec as P

NH = 64
KVH = 8
HD = 128
GROUP = NH // KVH
THETA = 500000.0
EPS = 1e-05
NEG = -1e30
LEAST = -1e29
MESH = pl.DeviceIdType.MESH
F32 = jnp.float32
BF16 = jnp.bfloat16
NEAR = 2
WIDE = 8
TOGETHER = 2


def layer_kernel(
    n,
    sections,
    lengths_hbm,
    entering_ref,
    newcomer_ref,
    gain_hbm,
    query_hbm,
    keyvalue_hbm,
    keys_hbm,
    values_hbm,
    out_ref,
    query_w,
    keyvalue_w,
    gain,
    inputs,
    normed,
    own_heads_out,
    heads,
    fresh_out,
    fresh_heads,
    staged,
    parts,
    leaving,
    load_sem,
    weight_sem,
    cache_sem,
    cache_send,
    send_sem,
    recv_sem,
    heads_sem,
    ready_sem,
    bias_near,
    bias_wide,
    keys_near,
    values_near,
    keys_wide,
    values_wide,
    lengths_ref,
):
    ticks, rows, width = out_ref.shape
    features = query_w.shape[0]
    own_heads = NH // n
    own_rows = own_heads * rows
    kv_width = keyvalue_w.shape[1]
    pieces = HD // kv_width
    per_group = n // KVH
    span = keys_hbm.shape[1] // rows
    chunks = weight_sem.shape[0] - 1
    depth = features // chunks
    scale = 1.0 / math.sqrt(HD)
    stride = HD // own_heads

    section = lax.axis_index("section")
    me = lax.axis_index("kvp")

    own_group = me // per_group

    def peer(step, skip):
        j = jnp.where(me >= n // 2, step, n - 1 - skip - step)
        return j + (j >= me).astype(jnp.int32) if skip else j

    barrier = pltpu.get_barrier_semaphore()

    def greet(step, carry):
        pl.semaphore_signal(
            barrier, inc=1, device_id=(section, peer(step, 1)), device_id_type=MESH
        )
        return carry

    lax.fori_loop(0, n - 1, greet, 0)
    if sections > 1:

        @pl.when(section < sections - 1)
        def _():
            pl.semaphore_signal(barrier, inc=1, device_id=(section + 1, me), device_id_type=MESH)

        @pl.when(section > 0)
        def _():
            pl.semaphore_signal(barrier, inc=1, device_id=(section - 1, me), device_id_type=MESH)

    lengths_load = pltpu.make_async_copy(lengths_hbm, lengths_ref, load_sem.at[2])
    lengths_load.start()
    own_load = pltpu.make_async_copy(entering_ref, inputs.at[0, me], load_sem.at[1])
    own_load.start()
    weight_loads = []
    for c in range(chunks):
        part = pl.ds(c * depth, depth)
        weight_loads.append(
            pltpu.make_async_copy(query_hbm.at[part], query_w.at[part], weight_sem.at[c])
        )
        weight_loads[-1].start()
    gain_load = pltpu.make_async_copy(gain_hbm, gain, load_sem.at[0])
    gain_load.start()
    weight_loads.append(pltpu.make_async_copy(keyvalue_hbm, keyvalue_w, weight_sem.at[chunks]))
    weight_loads[-1].start()

    neighbours = (section > 0).astype(jnp.int32) + (section < sections - 1).astype(jnp.int32)
    pl.semaphore_wait(barrier, n - 1 + neighbours)
    if sections > 1:

        @pl.when(section > 0)
        def _():
            pl.semaphore_signal(ready_sem, inc=1, device_id=(section - 1, me), device_id_type=MESH)

    def remote(source, target, sent, received, to_section, to):
        return pltpu.make_async_remote_copy(
            src_ref=source,
            dst_ref=target,
            send_sem=sent,
            recv_sem=received,
            device_id=(to_section, to),
            device_id_type=MESH,
        )

    def deliver(source, target, sent, received, to):
        @pl.when(to != me)
        def _():
            remote(source, target, sent, received, section, to).start()

        @pl.when(to == me)
        def _():
            pltpu.make_async_copy(source, target, received).start()

    def spread(source, target, sent, received):
        def send(step, carry):
            remote(source, target, sent, received, section, peer(step, 1)).start()
            return carry

        lax.fori_loop(0, n - 1, send, 0)

    def arrived(buffer, count, sem):
        if count:
            whole = buffer.at[pl.ds(0, count)]
            pltpu.make_async_copy(whole, whole, sem).wait()

    def all_sent(buffer, count, at_home, sem):
        @pl.when(at_home)
        def _():
            arrived(buffer, count - 1, sem)

        @pl.when(jnp.logical_not(at_home))
        def _():
            arrived(buffer, count, sem)

    def crossed(i):
        return i // 4 * 4 + lax.rem(i, 2) * 2 + lax.rem(i // 2, 2)

    def group_of(member, i, split):
        return crossed(member) if split == KVH else member * (KVH // split) + i

    def member_of(group, split):
        return crossed(group) if split == KVH else group // (KVH // split)

    def owner_slot(group, split):
        return lax.rem(group, KVH // split)

    def cache_of(t, split):
        if split == NEAR:
            return keys_near.at[t], values_near.at[t], bias_near.at[t]
        return keys_wide.at[t - 1], values_wide.at[t - 1], bias_wide.at[t - 1]

    def by_section(t, body):
        if t == 0:
            body(split=NEAR)
        else:
            pl.when(section == 0)(lambda: body(split=NEAR))
            if sections > 1:
                pl.when(section > 0)(lambda: body(split=WIDE))

    def deal_caches(t, split, kinds_now=(0, 1)):
        share = keys_hbm.shape[2] // split
        member = lax.rem(me, split)
        first = me - member
        for kind in kinds_now:
            source = (keys_hbm, values_hbm)[kind]
            target = cache_of(t, split)[kind]
            for i in range(1, split):
                other = lax.rem(member + i, split)
                columns = pl.ds(
                    pl.multiple_of(group_of(other, 0, split) * HD, HD), share
                )
                remote(
                    source.at[t, :, columns],
                    target.at[member],
                    cache_send.at[t, kind],
                    cache_sem.at[t, kind],
                    section,
                    first + other,
                ).start()
            columns = pl.ds(pl.multiple_of(group_of(member, 0, split) * HD, HD), share)
            pltpu.make_async_copy(
                source.at[t, :, columns], target.at[member], cache_sem.at[t, kind]
            ).start()

    spread(entering_ref, inputs.at[0, me], send_sem.at[0, 0], recv_sem.at[0, 0])

    @pl.when(section == 0)
    def _():
        for t in range(1, ticks):
            target = inputs.at[t, me]
            pltpu.make_async_copy(newcomer_ref.at[t - 1], target, recv_sem.at[t, 0]).start()
            spread(newcomer_ref.at[t - 1], target, send_sem.at[t, 0], recv_sem.at[t, 0])

    for t in range(ticks):
        by_section(t, functools.partial(deal_caches, t, kinds_now=(0, 1) if t == 0 else (0,)))

    lane = lax.broadcasted_iota(jnp.int32, (rows, HD), 1)
    half = HD // 2
    exponent = (lane % half).astype(F32) * (2.0 / HD)
    frequency = jnp.exp(exponent * (-math.log(THETA)))
    lengths_load.wait()

    def lengths_of(t, shape):
        request = lax.broadcasted_iota(jnp.int32, shape, 0)
        lengths = jnp.zeros(shape, jnp.int32)
        for b in range(rows):
            length = lengths_ref[t + sections - 1 - section, b]
            lengths = jnp.where(request == b, length, lengths)
        return request, lengths

    def put_bias(t, split):
        block, chunk = split * span, cache_of(t, split)[2].shape[1]
        request, limit = lengths_of(t, (rows, chunk))
        place = lax.broadcasted_iota(jnp.int32, (rows, chunk), 1)
        slot = place % block // span
        position = (me // split * split + slot) * span + place % span
        valid = (place // block == request % (chunk // block)) & (position < limit)
        cache_of(t, split)[2][...] = jnp.where(valid, 0.0, NEG).astype(F32)

    turns = []
    for t in range(ticks):
        angles = lengths_of(t, (rows, HD))[1].astype(F32) * frequency
        sine = jnp.sin(angles)
        turns.append((jnp.cos(angles), jnp.where(lane < half, -sine, sine)))
        by_section(t, functools.partial(put_bias, t))

    def rotated(head, t):
        cosine, sine = turns[t]
        return head * cosine + pltpu.roll(head, half, 1) * sine

    def packed(tops, totals):
        p = jnp.zeros((rows, HD), F32)
        for h in range(own_heads):
            p = jnp.where(lane == h * stride, tops[h], p)
            if totals is not None:
                p = jnp.where(lane == h * stride + 3, totals[h], p)
        return p

    kinds = n // 2
    fresh_group = (me % kinds) // pieces
    fresh_slot = (me // kinds) * pieces + me % pieces

    def find_query(t):
        if t == 0:
            own_load.wait()
            arrived(inputs.at[0], n - 1, recv_sem.at[0, 0])
        else:
            arrived(inputs.at[t], n, recv_sem.at[t, 0])

        squares = jnp.zeros((rows, width), F32)
        for s in range(n):
            x = inputs[t, s].astype(F32)
            squares = squares + x * x
        mean_square = jnp.sum(squares, axis=-1, keepdims=True) * (1.0 / features)
        factor = lax.rsqrt(mean_square + EPS)
        for s in range(n):
            part = pl.ds(s * width, width)
            x = inputs[t, s].astype(F32)
            normed[:, part] = (x * factor * gain[:, part].astype(F32)).astype(BF16)

        query = jnp.zeros((rows, width), F32)
        for c in range(chunks):
            part = pl.ds(c * depth, depth)
            if t == 0:
                weight_loads[c].wait()
            query = query + jnp.dot(normed[:, part], query_w[part], preferred_element_type=F32)
        own_query = jnp.concatenate(
            [rotated(query[:, h * HD : (h + 1) * HD], t) for h in range(own_heads)], axis=0
        ).astype(BF16)
        own_heads_out[t] = own_query

    def send_query(t, split):
        owners = n // split
        cluster = me // split
        home = member_of(own_group, split)
        slot = owner_slot(own_group, split) * per_group + lax.rem(me, per_group)

        def send(step, carry):
            to = jnp.where(cluster >= owners // 2, step, owners - 1 - step) * split + home
            deliver(
                own_heads_out.at[t],
                heads.at[t, slot],
                send_sem.at[t, 1],
                heads_sem.at[t, slot // per_group],
                to,
            )
            return carry

        lax.fori_loop(0, owners, send, 0)

    def find_fresh(t):
        if t == 0:
            weight_loads[chunks].wait()
        fresh = jnp.dot(normed[...], keyvalue_w[...], preferred_element_type=F32).astype(BF16)
        if pieces > 1:
            fresh = jnp.concatenate([fresh.astype(F32)] * pieces, axis=1)
            fresh = jnp.where(lane // kv_width == me % pieces, fresh, 0.0).astype(BF16)
        fresh_out[t] = fresh

    def send_fresh(t):
        for j in range(per_group):
            deliver(
                fresh_out.at[t],
                fresh_heads.at[t, fresh_slot],
                send_sem.at[t, 4],
                recv_sem.at[t, 1],
                fresh_group * per_group + j,
            )

    gain_load.wait()
    find_query(0)
    send_query(0, NEAR)
    for t in range(1, ticks):
        by_section(t, functools.partial(deal_caches, t, kinds_now=(1,)))
    find_fresh(0)
    send_fresh(0)

    @pl.when(section == 0)
    def _():
        for t in range(1, ticks):
            find_query(t)
            send_query(t, NEAR)
            find_fresh(t)
            send_fresh(t)

    for t in range(ticks):
        def attend(split):
            owners = n // split
            held = KVH // split
            member = lax.rem(me, split)
            cluster = me // split
            keys, values, bias_ref = cache_of(t, split)
            arrived(keys, split, cache_sem.at[t, 0])
            bias = bias_ref[...]
            block, chunk = split * span, bias.shape[1]
            per = chunk // block
            request = lax.broadcasted_iota(jnp.int32, (rows, chunk), 0)

            def chunk_of(cache, v, columns):
                return jnp.concatenate(
                    [
                        cache[:, b * span : (b + 1) * span, columns].reshape(block, HD)
                        for b in range(v * per, (v + 1) * per)
                    ],
                    axis=0,
                )

            def one_head(kv):
                queries = jnp.concatenate(
                    [heads[t, kv * per_group + j].astype(F32) for j in range(per_group)], axis=0
                ).astype(BF16)
                columns = pl.ds(pl.multiple_of(kv * HD, HD), HD)
                scores = None
                for v in range(rows // per):
                    part = lax.dot_general(
                        queries,
                        chunk_of(keys, v, columns),
                        (((1,), (1,)), ((), ())),
                        preferred_element_type=F32,
                    ).reshape(GROUP, rows, chunk)
                    scores = part if v == 0 else jnp.where(request // per == v, part, scores)
                scores = scores * scale + bias
                top = jnp.maximum(jnp.max(scores, axis=-1, keepdims=True), LEAST)
                weights = jnp.exp(scores - top)
                total = jnp.sum(weights, axis=-1, keepdims=True)
                weighted = jnp.zeros((GROUP * rows, HD), F32)
                for v in range(rows // per):
                    weighted = weighted + jnp.dot(
                        jnp.where(request // per == v, weights, 0.0)
                        .reshape(GROUP * rows, chunk)
                        .astype(BF16),
                        chunk_of(values, v, columns),
                        preferred_element_type=F32,
                    )
                return top, total, weighted

            arrived(values, split, cache_sem.at[t, 1])
            ordered = [
                jnp.where(me >= group_of(member, held // 2, split) * per_group, held - 1 - i, i)
                for i in range(held)
            ]
            for i in range(0, held, TOGETHER):
                some = ordered[i : i + TOGETHER]
                for kv in some:
                    arrived(heads.at[t], per_group, heads_sem.at[t, kv])
                found = [one_head(kv) for kv in some]
                for kv, (top, total, weighted) in zip(some, found):
                    for j in range(per_group):
                        these = slice(j * own_heads, (j + 1) * own_heads)
                        stats = packed(top[these], total[these])
                        high = stats.astype(BF16).astype(F32)
                        rest = stats - high
                        middle = rest.astype(BF16).astype(F32)
                        stats = high + pltpu.roll(middle, 1, 1) + pltpu.roll(rest - middle, 2, 1)
                        place = kv * per_group + j
                        staged[t, place] = jnp.concatenate(
                            [weighted[j * own_rows : (j + 1) * own_rows], stats], axis=0
                        ).astype(BF16)
                        deliver(
                            staged.at[t, place],
                            parts.at[t, cluster],
                            send_sem.at[t, 2],
                            recv_sem.at[t, 2],
                            group_of(member, kv, split) * per_group + j,
                        )

        by_section(t, attend)

        arrived(fresh_heads.at[t], 2 * pieces, recv_sem.at[t, 1])
        own_query = own_heads_out[t].astype(F32)
        new_key = jnp.zeros((rows, HD), F32)
        new_value = jnp.zeros((rows, HD), F32)
        for j in range(pieces):
            new_key = new_key + fresh_heads[t, j].astype(F32)
            new_value = new_value + fresh_heads[t, pieces + j].astype(F32)
        new_key = rotated(new_key, t)
        new_score = packed(
            [
                jnp.sum(own_query[h * rows : (h + 1) * rows] * new_key, axis=-1, keepdims=True)
                * scale
                for h in range(own_heads)
            ],
            None,
        )

        def combine(split):
            owners = n // split
            arrived(parts.at[t], owners, recv_sem.at[t, 2])
            sums = []
            blocks = []
            for s in range(owners):
                block = parts[t, s].astype(F32)
                blocks.append(block)
                stats = block[own_rows : own_rows + rows]
                sums.append(stats + pltpu.roll(stats, HD - 1, 1) + pltpu.roll(stats, HD - 2, 1))
            top = new_score
            for s in range(owners):
                top = jnp.maximum(top, sums[s])
            new_weight = jnp.exp(new_score - top)
            denominator = new_weight
            factors = []
            for s in range(owners):
                factors.append(jnp.exp(sums[s] - top))
                denominator = denominator + factors[s] * pltpu.roll(sums[s], HD - 3, 1)
            inverse = 1.0 / denominator
            attended = []
            for h in range(own_heads):
                at = slice(h * stride, h * stride + 1)
                total = (new_weight * inverse)[:, at] * new_value
                for s in range(owners):
                    total = total + (factors[s] * inverse)[:, at] * blocks[s][h * rows : (h + 1) * rows]
                attended.append(total)
            attended = jnp.concatenate(attended, axis=1)
            result = (inputs[t, me].astype(F32) + attended).astype(BF16)
            out_ref[t] = result

        by_section(t, combine)
        if t < ticks - 1 and sections > 1:
            leaving[t] = out_ref[t]

            @pl.when(section < sections - 1)
            def _():
                if t == 0:
                    pl.semaphore_wait(ready_sem, 1)

                def send(step, carry):
                    remote(
                        leaving.at[t],
                        inputs.at[t + 1, me],
                        send_sem.at[t, 3],
                        recv_sem.at[t + 1, 0],
                        section + 1,
                        step,
                    ).start()
                    return carry

                lax.fori_loop(0, n, send, 0)

        if t < ticks - 1 and sections > 1:

            @pl.when(section > 0)
            def _():
                find_query(t + 1)
                send_query(t + 1, WIDE)
                find_fresh(t + 1)
                send_fresh(t + 1)

    for t in range(ticks):
        if t == 0:
            arrived(inputs.at[t], n - 1, send_sem.at[t, 0])
        else:

            @pl.when(section == 0)
            def _():
                arrived(inputs.at[t], n - 1, send_sem.at[t, 0])

        def settle(split):
            owners = n // split
            inside = lax.rem(me, split) == member_of(own_group, split)
            all_sent(heads.at[t], owners, inside, send_sem.at[t, 1])
            all_sent(parts.at[t], owners, inside, send_sem.at[t, 2])
            for kind in range(2):
                arrived(cache_of(t, split)[kind], split - 1, cache_send.at[t, kind])

        by_section(t, settle)
        all_sent(fresh_heads.at[t], per_group, fresh_group == own_group, send_sem.at[t, 4])
        if t < ticks - 1 and sections > 1:

            @pl.when(section < sections - 1)
            def _():
                arrived(inputs.at[t], n, send_sem.at[t, 3])


def shards(
    n,
    sections,
    entering,
    newcomer,
    norm_gain,
    query_weight,
    keyvalue_weight,
    key_cache,
    value_cache,
    cache_lengths,
):
    _, rows, width = entering.shape
    _, features, _ = query_weight.shape
    kv_width = keyvalue_weight.shape[2]
    _, ticks, _, span, kv_features = key_cache.shape
    own_rows = (NH // n) * rows
    pieces = HD // kv_width
    per_group = n // KVH
    chunks = 4
    most = n // NEAR
    later = max(ticks - 1, 1)
    anywhere = pl.BlockSpec(memory_space=pl.ANY)
    out = pl.pallas_call(
        functools.partial(layer_kernel, n, sections),
        out_shape=pltpu.VMEM((ticks, rows, width), BF16),
        in_specs=[anywhere] * 8,
        out_specs=pl.BlockSpec(memory_space=pltpu.VMEM),
        scratch_shapes=[
            pltpu.VMEM((features, width), BF16),
            pltpu.VMEM((features, kv_width), BF16),
            pltpu.VMEM((1, features), BF16),
            pltpu.VMEM((ticks, n, rows, width), BF16),
            pltpu.VMEM((rows, features), BF16),
            pltpu.VMEM((ticks, own_rows, HD), BF16),
            pltpu.VMEM((ticks, most, own_rows, HD), BF16),
            pltpu.VMEM((ticks, rows, HD), BF16),
            pltpu.VMEM((ticks, max(2 * pieces, per_group), rows, HD), BF16),
            pltpu.VMEM((ticks, most, own_rows + rows, HD), BF16),
            pltpu.VMEM((ticks, most, own_rows + rows, HD), BF16),
            pltpu.VMEM((ticks, rows, width), BF16),
            pltpu.SemaphoreType.DMA((3,)),
            pltpu.SemaphoreType.DMA((chunks + 1,)),
            pltpu.SemaphoreType.DMA((ticks, 2)),
            pltpu.SemaphoreType.DMA((ticks, 2)),
            pltpu.SemaphoreType.DMA((ticks, 5)),
            pltpu.SemaphoreType.DMA((ticks, 3)),
            pltpu.SemaphoreType.DMA((ticks, KVH // NEAR)),
            pltpu.SemaphoreType.REGULAR,
            pltpu.VMEM((ticks, rows, max(NEAR * span, HD)), F32),
            pltpu.VMEM((later, rows, max(WIDE * span, HD)), F32),
            pltpu.VMEM((ticks, NEAR, rows * span, kv_features // NEAR), BF16),
            pltpu.VMEM((ticks, NEAR, rows * span, kv_features // NEAR), BF16),
            pltpu.VMEM((later, WIDE, rows * span, kv_features // WIDE), BF16),
            pltpu.VMEM((later, WIDE, rows * span, kv_features // WIDE), BF16),
            pltpu.SMEM(cache_lengths.shape, jnp.int32),
        ],
        compiler_params=pltpu.CompilerParams(
            collective_id=0, has_side_effects=True, vmem_limit_bytes=60 << 20
        ),
    )(
        cache_lengths,
        entering[0],
        newcomer,
        norm_gain,
        query_weight[0],
        keyvalue_weight[0],
        key_cache.reshape(ticks, rows * span, kv_features),
        value_cache.reshape(ticks, rows * span, kv_features),
    )
    return out[None]


def solution(mesh):
    placed = (
        P("section", None, "kvp"),
        P(None, None, "kvp"),
        P("section", None),
        P("section", None, "kvp"),
        P("section", None, "kvp"),
        P("section", None, None, "kvp", None),
        P("section", None, None, "kvp", None),
        P(),
    )
    return jax.shard_map(
        functools.partial(shards, mesh.shape["kvp"], mesh.shape["section"]),
        mesh=mesh,
        in_specs=placed,
        out_specs=P("section", None, None, "kvp"),
        check_vma=False,
    )
```

```python
import functools
import math

import jax
import jax.numpy as jnp
from jax import lax
from jax.experimental import pallas as pl
from jax.experimental.pallas import tpu as pltpu
from jax.sharding import PartitionSpec as P

NH = 64
KVH = 8
HD = 128
GROUP = NH // KVH
THETA = 500000.0
EPS = 1e-05
NEG = -1e30
LEAST = -1e29
MESH = pl.DeviceIdType.MESH
F32 = jnp.float32
BF16 = jnp.bfloat16
NEAR = 2
WIDE = 8
TOGETHER = 2


def layer_kernel(
    n,
    sections,
    lengths_hbm,
    entering_ref,
    newcomer_ref,
    gain_hbm,
    query_hbm,
    keyvalue_hbm,
    keys_hbm,
    values_hbm,
    out_ref,
    query_w,
    keyvalue_w,
    gain,
    inputs,
    normed,
    own_heads_out,
    heads,
    fresh_out,
    fresh_heads,
    staged,
    parts,
    leaving,
    load_sem,
    weight_sem,
    cache_sem,
    cache_send,
    send_sem,
    recv_sem,
    heads_sem,
    ready_sem,
    bias_near,
    bias_wide,
    keys_near,
    values_near,
    keys_wide,
    values_wide,
    lengths_ref,
):
    ticks, rows, width = out_ref.shape
    features = query_w.shape[0]
    own_heads = NH // n
    own_rows = own_heads * rows
    kv_width = keyvalue_w.shape[1]
    pieces = HD // kv_width
    per_group = n // KVH
    span = keys_hbm.shape[1] // rows
    chunks = weight_sem.shape[0] - 1
    depth = features // chunks
    scale = 1.0 / math.sqrt(HD)
    stride = HD // own_heads

    section = lax.axis_index("section")
    me = lax.axis_index("kvp")

    own_group = me // per_group

    def peer(step, skip):
        j = jnp.where(me >= n // 2, step, n - 1 - skip - step)
        return j + (j >= me).astype(jnp.int32) if skip else j

    barrier = pltpu.get_barrier_semaphore()

    def greet(step, carry):
        pl.semaphore_signal(
            barrier, inc=1, device_id=(section, peer(step, 1)), device_id_type=MESH
        )
        return carry

    lax.fori_loop(0, n - 1, greet, 0)
    if sections > 1:

        @pl.when(section < sections - 1)
        def _():
            pl.semaphore_signal(barrier, inc=1, device_id=(section + 1, me), device_id_type=MESH)

        @pl.when(section > 0)
        def _():
            pl.semaphore_signal(barrier, inc=1, device_id=(section - 1, me), device_id_type=MESH)

    lengths_load = pltpu.make_async_copy(lengths_hbm, lengths_ref, load_sem.at[2])
    lengths_load.start()
    own_load = pltpu.make_async_copy(entering_ref, inputs.at[0, me], load_sem.at[1])
    own_load.start()
    weight_loads = []
    for c in range(chunks):
        part = pl.ds(c * depth, depth)
        weight_loads.append(
            pltpu.make_async_copy(query_hbm.at[part], query_w.at[part], weight_sem.at[c])
        )
        weight_loads[-1].start()
    gain_load = pltpu.make_async_copy(gain_hbm, gain, load_sem.at[0])
    gain_load.start()
    weight_loads.append(pltpu.make_async_copy(keyvalue_hbm, keyvalue_w, weight_sem.at[chunks]))
    weight_loads[-1].start()

    neighbours = (section > 0).astype(jnp.int32) + (section < sections - 1).astype(jnp.int32)
    pl.semaphore_wait(barrier, n - 1 + neighbours)
    if sections > 1:

        @pl.when(section > 0)
        def _():
            pl.semaphore_signal(ready_sem, inc=1, device_id=(section - 1, me), device_id_type=MESH)

    def remote(source, target, sent, received, to_section, to):
        return pltpu.make_async_remote_copy(
            src_ref=source,
            dst_ref=target,
            send_sem=sent,
            recv_sem=received,
            device_id=(to_section, to),
            device_id_type=MESH,
        )

    def deliver(source, target, sent, received, to):
        @pl.when(to != me)
        def _():
            remote(source, target, sent, received, section, to).start()

        @pl.when(to == me)
        def _():
            pltpu.make_async_copy(source, target, received).start()

    def spread(source, target, sent, received):
        def send(step, carry):
            remote(source, target, sent, received, section, peer(step, 1)).start()
            return carry

        lax.fori_loop(0, n - 1, send, 0)

    def arrived(buffer, count, sem):
        if count:
            whole = buffer.at[pl.ds(0, count)]
            pltpu.make_async_copy(whole, whole, sem).wait()

    def all_sent(buffer, count, at_home, sem):
        @pl.when(at_home)
        def _():
            arrived(buffer, count - 1, sem)

        @pl.when(jnp.logical_not(at_home))
        def _():
            arrived(buffer, count, sem)

    def crossed(i):
        return i // 4 * 4 + lax.rem(i, 2) * 2 + lax.rem(i // 2, 2)

    def group_of(member, i, split):
        return crossed(member) if split == KVH else member * (KVH // split) + i

    def member_of(group, split):
        return crossed(group) if split == KVH else group // (KVH // split)

    def owner_slot(group, split):
        return lax.rem(group, KVH // split)

    def cache_of(t, split):
        if split == NEAR:
            return keys_near.at[t], values_near.at[t], bias_near.at[t]
        return keys_wide.at[t - 1], values_wide.at[t - 1], bias_wide.at[t - 1]

    def by_section(t, body):
        if t == 0:
            body(split=NEAR)
        else:
            pl.when(section == 0)(lambda: body(split=NEAR))
            if sections > 1:
                pl.when(section > 0)(lambda: body(split=WIDE))

    def deal_caches(t, split, kinds_now=(0, 1)):
        share = keys_hbm.shape[2] // split
        member = lax.rem(me, split)
        first = me - member
        for kind in kinds_now:
            source = (keys_hbm, values_hbm)[kind]
            target = cache_of(t, split)[kind]
            for i in range(1, split):
                other = lax.rem(member + i, split)
                columns = pl.ds(
                    pl.multiple_of(group_of(other, 0, split) * HD, HD), share
                )
                remote(
                    source.at[t, :, columns],
                    target.at[member],
                    cache_send.at[t, kind],
                    cache_sem.at[t, kind],
                    section,
                    first + other,
                ).start()
            columns = pl.ds(pl.multiple_of(group_of(member, 0, split) * HD, HD), share)
            pltpu.make_async_copy(
                source.at[t, :, columns], target.at[member], cache_sem.at[t, kind]
            ).start()

    spread(entering_ref, inputs.at[0, me], send_sem.at[0, 0], recv_sem.at[0, 0])

    @pl.when(section == 0)
    def _():
        for t in range(1, ticks):
            target = inputs.at[t, me]
            pltpu.make_async_copy(newcomer_ref.at[t - 1], target, recv_sem.at[t, 0]).start()
            spread(newcomer_ref.at[t - 1], target, send_sem.at[t, 0], recv_sem.at[t, 0])

    for t in range(ticks):
        by_section(t, functools.partial(deal_caches, t, kinds_now=(0, 1) if t == 0 else (0,)))

    lane = lax.broadcasted_iota(jnp.int32, (rows, HD), 1)
    half = HD // 2
    exponent = (lane % half).astype(F32) * (2.0 / HD)
    frequency = jnp.exp(exponent * (-math.log(THETA)))
    lengths_load.wait()

    def lengths_of(t, shape):
        request = lax.broadcasted_iota(jnp.int32, shape, 0)
        lengths = jnp.zeros(shape, jnp.int32)
        for b in range(rows):
            length = lengths_ref[t + sections - 1 - section, b]
            lengths = jnp.where(request == b, length, lengths)
        return request, lengths

    def put_bias(t, split):
        block, chunk = split * span, cache_of(t, split)[2].shape[1]
        request, limit = lengths_of(t, (rows, chunk))
        place = lax.broadcasted_iota(jnp.int32, (rows, chunk), 1)
        slot = place % block // span
        position = (me // split * split + slot) * span + place % span
        valid = (place // block == request % (chunk // block)) & (position < limit)
        cache_of(t, split)[2][...] = jnp.where(valid, 0.0, NEG).astype(F32)

    turns = []
    for t in range(ticks):
        angles = lengths_of(t, (rows, HD))[1].astype(F32) * frequency
        sine = jnp.sin(angles)
        turns.append((jnp.cos(angles), jnp.where(lane < half, -sine, sine)))
        by_section(t, functools.partial(put_bias, t))

    def rotated(head, t):
        cosine, sine = turns[t]
        return head * cosine + pltpu.roll(head, half, 1) * sine

    def packed(tops, totals):
        p = jnp.zeros((rows, HD), F32)
        for h in range(own_heads):
            p = jnp.where(lane == h * stride, tops[h], p)
            if totals is not None:
                p = jnp.where(lane == h * stride + 3, totals[h], p)
        return p

    kinds = n // 2
    fresh_group = (me % kinds) // pieces
    fresh_slot = (me // kinds) * pieces + me % pieces

    def find_query(t):
        if t == 0:
            own_load.wait()
            arrived(inputs.at[0], n - 1, recv_sem.at[0, 0])
        else:
            arrived(inputs.at[t], n, recv_sem.at[t, 0])

        squares = jnp.zeros((rows, width), F32)
        for s in range(n):
            x = inputs[t, s].astype(F32)
            squares = squares + x * x
        mean_square = jnp.sum(squares, axis=-1, keepdims=True) * (1.0 / features)
        factor = lax.rsqrt(mean_square + EPS)
        for s in range(n):
            part = pl.ds(s * width, width)
            x = inputs[t, s].astype(F32)
            normed[:, part] = (x * factor * gain[:, part].astype(F32)).astype(BF16)

        query = jnp.zeros((rows, width), F32)
        for c in range(chunks):
            part = pl.ds(c * depth, depth)
            if t == 0:
                weight_loads[c].wait()
            query = query + jnp.dot(normed[:, part], query_w[part], preferred_element_type=F32)
        own_query = jnp.concatenate(
            [rotated(query[:, h * HD : (h + 1) * HD], t) for h in range(own_heads)], axis=0
        ).astype(BF16)
        own_heads_out[t] = own_query

    def send_query(t, split):
        owners = n // split
        cluster = me // split
        home = member_of(own_group, split)
        slot = owner_slot(own_group, split) * per_group + lax.rem(me, per_group)

        def send(step, carry):
            to = jnp.where(cluster >= owners // 2, step, owners - 1 - step) * split + home
            deliver(
                own_heads_out.at[t],
                heads.at[t, slot],
                send_sem.at[t, 1],
                heads_sem.at[t, slot // per_group],
                to,
            )
            return carry

        lax.fori_loop(0, owners, send, 0, unroll=2)

    def find_fresh(t):
        if t == 0:
            weight_loads[chunks].wait()
        fresh = jnp.dot(normed[...], keyvalue_w[...], preferred_element_type=F32).astype(BF16)
        if pieces > 1:
            fresh = jnp.concatenate([fresh.astype(F32)] * pieces, axis=1)
            fresh = jnp.where(lane // kv_width == me % pieces, fresh, 0.0).astype(BF16)
        fresh_out[t] = fresh

    def send_fresh(t):
        for j in range(per_group):
            deliver(
                fresh_out.at[t],
                fresh_heads.at[t, fresh_slot],
                send_sem.at[t, 4],
                recv_sem.at[t, 1],
                fresh_group * per_group + j,
            )

    gain_load.wait()
    find_query(0)
    send_query(0, NEAR)
    for t in range(1, ticks):
        by_section(t, functools.partial(deal_caches, t, kinds_now=(1,)))
    find_fresh(0)
    send_fresh(0)

    @pl.when(section == 0)
    def _():
        for t in range(1, ticks):
            find_query(t)
            send_query(t, NEAR)
            find_fresh(t)
            send_fresh(t)

    for t in range(ticks):
        def attend(split):
            owners = n // split
            held = KVH // split
            member = lax.rem(me, split)
            cluster = me // split
            keys, values, bias_ref = cache_of(t, split)
            arrived(keys, split, cache_sem.at[t, 0])
            bias = bias_ref[...]
            block, chunk = split * span, bias.shape[1]
            per = chunk // block
            request = lax.broadcasted_iota(jnp.int32, (rows, chunk), 0)

            def chunk_of(cache, v, columns):
                return jnp.concatenate(
                    [
                        cache[:, b * span : (b + 1) * span, columns].reshape(block, HD)
                        for b in range(v * per, (v + 1) * per)
                    ],
                    axis=0,
                )

            def one_head(kv):
                queries = jnp.concatenate(
                    [heads[t, kv * per_group + j].astype(F32) for j in range(per_group)], axis=0
                ).astype(BF16)
                columns = pl.ds(pl.multiple_of(kv * HD, HD), HD)
                scores = None
                for v in range(rows // per):
                    part = lax.dot_general(
                        queries,
                        chunk_of(keys, v, columns),
                        (((1,), (1,)), ((), ())),
                        preferred_element_type=F32,
                    ).reshape(GROUP, rows, chunk)
                    scores = part if v == 0 else jnp.where(request // per == v, part, scores)
                scores = scores * scale + bias
                top = jnp.maximum(jnp.max(scores, axis=-1, keepdims=True), LEAST)
                weights = jnp.exp(scores - top)
                total = jnp.sum(weights, axis=-1, keepdims=True)
                weighted = jnp.zeros((GROUP * rows, HD), F32)
                for v in range(rows // per):
                    weighted = weighted + jnp.dot(
                        jnp.where(request // per == v, weights, 0.0)
                        .reshape(GROUP * rows, chunk)
                        .astype(BF16),
                        chunk_of(values, v, columns),
                        preferred_element_type=F32,
                    )
                return top, total, weighted

            arrived(values, split, cache_sem.at[t, 1])
            ordered = [
                jnp.where(me >= group_of(member, held // 2, split) * per_group, held - 1 - i, i)
                for i in range(held)
            ]
            for i in range(0, held, TOGETHER):
                some = ordered[i : i + TOGETHER]
                for kv in some:
                    arrived(heads.at[t], per_group, heads_sem.at[t, kv])
                found = [one_head(kv) for kv in some]
                for kv, (top, total, weighted) in zip(some, found):
                    for j in range(per_group):
                        these = slice(j * own_heads, (j + 1) * own_heads)
                        stats = packed(top[these], total[these])
                        high = stats.astype(BF16).astype(F32)
                        rest = stats - high
                        middle = rest.astype(BF16).astype(F32)
                        stats = high + pltpu.roll(middle, 1, 1) + pltpu.roll(rest - middle, 2, 1)
                        place = kv * per_group + j
                        staged[t, place] = jnp.concatenate(
                            [weighted[j * own_rows : (j + 1) * own_rows], stats], axis=0
                        ).astype(BF16)
                        deliver(
                            staged.at[t, place],
                            parts.at[t, cluster],
                            send_sem.at[t, 2],
                            recv_sem.at[t, 2],
                            group_of(member, kv, split) * per_group + j,
                        )

        by_section(t, attend)

        arrived(fresh_heads.at[t], 2 * pieces, recv_sem.at[t, 1])
        own_query = own_heads_out[t].astype(F32)
        new_key = jnp.zeros((rows, HD), F32)
        new_value = jnp.zeros((rows, HD), F32)
        for j in range(pieces):
            new_key = new_key + fresh_heads[t, j].astype(F32)
            new_value = new_value + fresh_heads[t, pieces + j].astype(F32)
        new_key = rotated(new_key, t)
        new_score = packed(
            [
                jnp.sum(own_query[h * rows : (h + 1) * rows] * new_key, axis=-1, keepdims=True)
                * scale
                for h in range(own_heads)
            ],
            None,
        )

        def combine(split):
            owners = n // split
            arrived(parts.at[t], owners, recv_sem.at[t, 2])
            sums = []
            blocks = []
            for s in range(owners):
                block = parts[t, s].astype(F32)
                blocks.append(block)
                stats = block[own_rows : own_rows + rows]
                sums.append(stats + pltpu.roll(stats, HD - 1, 1) + pltpu.roll(stats, HD - 2, 1))
            top = new_score
            for s in range(owners):
                top = jnp.maximum(top, sums[s])
            new_weight = jnp.exp(new_score - top)
            denominator = new_weight
            factors = []
            for s in range(owners):
                factors.append(jnp.exp(sums[s] - top))
                denominator = denominator + factors[s] * pltpu.roll(sums[s], HD - 3, 1)
            inverse = 1.0 / denominator
            attended = []
            for h in range(own_heads):
                at = slice(h * stride, h * stride + 1)
                total = (new_weight * inverse)[:, at] * new_value
                for s in range(owners):
                    total = total + (factors[s] * inverse)[:, at] * blocks[s][h * rows : (h + 1) * rows]
                attended.append(total)
            attended = jnp.concatenate(attended, axis=1)
            result = (inputs[t, me].astype(F32) + attended).astype(BF16)
            out_ref[t] = result

        by_section(t, combine)
        if t < ticks - 1 and sections > 1:
            leaving[t] = out_ref[t]

            @pl.when(section < sections - 1)
            def _():
                if t == 0:
                    pl.semaphore_wait(ready_sem, 1)

                def send(step, carry):
                    remote(
                        leaving.at[t],
                        inputs.at[t + 1, me],
                        send_sem.at[t, 3],
                        recv_sem.at[t + 1, 0],
                        section + 1,
                        step,
                    ).start()
                    return carry

                lax.fori_loop(0, n, send, 0, unroll=4)

        if t < ticks - 1 and sections > 1:

            @pl.when(section > 0)
            def _():
                find_query(t + 1)
                send_query(t + 1, WIDE)
                find_fresh(t + 1)
                send_fresh(t + 1)

    for t in range(ticks):
        if t == 0:
            arrived(inputs.at[t], n - 1, send_sem.at[t, 0])
        else:

            @pl.when(section == 0)
            def _():
                arrived(inputs.at[t], n - 1, send_sem.at[t, 0])

        def settle(split):
            owners = n // split
            inside = lax.rem(me, split) == member_of(own_group, split)
            all_sent(heads.at[t], owners, inside, send_sem.at[t, 1])
            all_sent(parts.at[t], owners, inside, send_sem.at[t, 2])
            for kind in range(2):
                arrived(cache_of(t, split)[kind], split - 1, cache_send.at[t, kind])

        by_section(t, settle)
        all_sent(fresh_heads.at[t], per_group, fresh_group == own_group, send_sem.at[t, 4])
        if t < ticks - 1 and sections > 1:

            @pl.when(section < sections - 1)
            def _():
                arrived(inputs.at[t], n, send_sem.at[t, 3])


def shards(
    n,
    sections,
    entering,
    newcomer,
    norm_gain,
    query_weight,
    keyvalue_weight,
    key_cache,
    value_cache,
    cache_lengths,
):
    _, rows, width = entering.shape
    _, features, _ = query_weight.shape
    kv_width = keyvalue_weight.shape[2]
    _, ticks, _, span, kv_features = key_cache.shape
    own_rows = (NH // n) * rows
    pieces = HD // kv_width
    per_group = n // KVH
    chunks = 4
    most = n // NEAR
    later = max(ticks - 1, 1)
    anywhere = pl.BlockSpec(memory_space=pl.ANY)
    out = pl.pallas_call(
        functools.partial(layer_kernel, n, sections),
        out_shape=pltpu.VMEM((ticks, rows, width), BF16),
        in_specs=[anywhere] * 8,
        out_specs=pl.BlockSpec(memory_space=pltpu.VMEM),
        scratch_shapes=[
            pltpu.VMEM((features, width), BF16),
            pltpu.VMEM((features, kv_width), BF16),
            pltpu.VMEM((1, features), BF16),
            pltpu.VMEM((ticks, n, rows, width), BF16),
            pltpu.VMEM((rows, features), BF16),
            pltpu.VMEM((ticks, own_rows, HD), BF16),
            pltpu.VMEM((ticks, most, own_rows, HD), BF16),
            pltpu.VMEM((ticks, rows, HD), BF16),
            pltpu.VMEM((ticks, max(2 * pieces, per_group), rows, HD), BF16),
            pltpu.VMEM((ticks, most, own_rows + rows, HD), BF16),
            pltpu.VMEM((ticks, most, own_rows + rows, HD), BF16),
            pltpu.VMEM((ticks, rows, width), BF16),
            pltpu.SemaphoreType.DMA((3,)),
            pltpu.SemaphoreType.DMA((chunks + 1,)),
            pltpu.SemaphoreType.DMA((ticks, 2)),
            pltpu.SemaphoreType.DMA((ticks, 2)),
            pltpu.SemaphoreType.DMA((ticks, 5)),
            pltpu.SemaphoreType.DMA((ticks, 3)),
            pltpu.SemaphoreType.DMA((ticks, KVH // NEAR)),
            pltpu.SemaphoreType.REGULAR,
            pltpu.VMEM((ticks, rows, max(NEAR * span, HD)), F32),
            pltpu.VMEM((later, rows, max(WIDE * span, HD)), F32),
            pltpu.VMEM((ticks, NEAR, rows * span, kv_features // NEAR), BF16),
            pltpu.VMEM((ticks, NEAR, rows * span, kv_features // NEAR), BF16),
            pltpu.VMEM((later, WIDE, rows * span, kv_features // WIDE), BF16),
            pltpu.VMEM((later, WIDE, rows * span, kv_features // WIDE), BF16),
            pltpu.SMEM(cache_lengths.shape, jnp.int32),
        ],
        compiler_params=pltpu.CompilerParams(
            collective_id=0, has_side_effects=True, vmem_limit_bytes=60 << 20
        ),
    )(
        cache_lengths,
        entering[0],
        newcomer,
        norm_gain,
        query_weight[0],
        keyvalue_weight[0],
        key_cache.reshape(ticks, rows * span, kv_features),
        value_cache.reshape(ticks, rows * span, kv_features),
    )
    return out[None]


def solution(mesh):
    placed = (
        P("section", None, "kvp"),
        P(None, None, "kvp"),
        P("section", None),
        P("section", None, "kvp"),
        P("section", None, "kvp"),
        P("section", None, None, "kvp", None),
        P("section", None, None, "kvp", None),
        P(),
    )
    return jax.shard_map(
        functools.partial(shards, mesh.shape["kvp"], mesh.shape["section"]),
        mesh=mesh,
        in_specs=placed,
        out_specs=P("section", None, None, "kvp"),
        check_vma=False,
    )
```
